32 devices in a mesh: gx: 8 (over z, x), gy: 4 (over y, core).
Axes of the slice: x: 2, y: 2, z: 4, core: 2. Of those that a mesh axis runs over, the one named last changes fastest.
Arguments:
- site_frac: float32 [3, 16, 8, 128], P(None, 'gx', 'gy'), may hold values from 0 to 1
- dual_weight: float32 [16, 8, 128], P('gx', 'gy'), may hold values from -2.5 to 64
- target_mass: float32 [16, 8, 128], P('gx', 'gy'), may hold values from 0.2 to 0.8
- block_list: int32 [8, 4, 12], P('gx', 'gy'), may hold values from 0 to 35, as said below
- block_count: int32 [8, 4], P('gx', 'gy'), may hold values from 1 to 12, as said below
Outputs:
- new_dual: float32 [16, 8, 128], P('gx', 'gy')
- site_shift: float32 [3, 16, 8, 128], P(None, 'gx', 'gy')
- displacement: float32 [3, 32, 16, 256], P(None, 'gx', 'gy')
The draws below stay inside these ranges and needn't reach their ends.
Inputs may be any that keep to these rules, and one draw needn't show every extreme that they name: `block_list`: within one tile the 12 entries are distinct. The first block_count entries name halo slots whose blocks hold sites of that tile's neighbourhood. `block_count`: some tile uses all 12 entries.
All inputs are finite; a program needn't handle non-finite values.
Results may differ from the reference program's by a relative error of at most 0.0003.
Values sent between devices are 32-bit elements; how exact they have to be, the bound alone decides.
A program may use at most 64 MiB of HBM per device.

```python
import jax
import jax.numpy as jnp
from jax import lax

TX = 4
TY = 4
Z = 256
SB_SIDE = 2
BLOCK = 128
K_MAX = 12
NBX = 16
NBY = 8
NX = 32
NY = 16
N_GX = 8
N_GY = 4


def layout_draw(key):
    base_key = jax.random.fold_in(key, 11)
    key_first = jax.random.fold_in(base_key, 0)
    key_pick = jax.random.fold_in(base_key, 2)
    key_order = jax.random.fold_in(base_key, 3)
    blocks = SB_SIDE * SB_SIDE
    lowest = blocks // 2
    living = jax.random.randint(key_first, (N_GX, N_GY), lowest, blocks + 1)
    chosen_tile = jax.random.randint(key_pick, (), 0, N_GX * N_GY)
    tile_serial = jnp.arange(N_GX * N_GY).reshape(N_GX, N_GY)
    living = jnp.where(tile_serial == chosen_tile, blocks, living)
    span_slots = 3 * SB_SIDE
    slot_ids = jnp.arange(span_slots * span_slots)
    slot_row = slot_ids // span_slots
    slot_col = slot_ids % span_slots
    near_x = (jnp.arange(N_GX)[:, None, None] + slot_row[None, None, :] // SB_SIDE - 1) % N_GX
    near_y = (jnp.arange(N_GY)[None, :, None] + slot_col[None, None, :] // SB_SIDE - 1) % N_GY
    inner_id = slot_row % SB_SIDE * SB_SIDE + slot_col % SB_SIDE
    usable = (inner_id[None, None, :] < living[near_x, near_y]).astype(jnp.int32)
    ranking = jax.random.randint(key_order, (N_GX, N_GY, span_slots * span_slots), 0, 1024)
    keyed_rank = usable * (1024 * span_slots * span_slots) + ranking * (span_slots * span_slots) + slot_ids[None, None, :]
    ignored, chosen_order = lax.top_k(keyed_rank, K_MAX)
    available = jnp.sum(usable, axis=-1)
    counts = jnp.minimum(jnp.minimum(available, K_MAX), (K_MAX * living + blocks - 1) // blocks)
    return (chosen_order.astype(jnp.int32), counts.astype(jnp.int32))


def draw_block_list(key, part):
    return layout_draw(key)[0]


def draw_block_count(key, part):
    return layout_draw(key)[1]


def draw_dual_weight(key, part):
    key_base = jax.random.fold_in(jax.random.fold_in(key, 23), 0)
    dims_shape = (NBX, NBY, BLOCK)
    return jnp.clip(0.5 * jax.random.normal(key_base, dims_shape, jnp.float32), -2.5, 2.5)


def block_levels(own_key, extent, cuts, least, largest):
    level, own = 1.0, jax.random.fold_in(own_key, 6)
    for dim, blocks in cuts:
        draws = jnp.exp(jax.random.uniform(jax.random.fold_in(own, dim), (blocks,), jnp.float32, least / len(cuts), largest / len(cuts)))
        level = level * jnp.repeat(draws, extent[dim] // blocks).reshape([-1 if axis == dim else 1 for axis in range(len(extent))])
    return level


def setup_inputs(seed: int = 0) -> dict:
    keys = jax.random.split(jax.random.key(seed), 6)
    site_frac = jnp.clip(1.0 * jax.random.uniform(keys[0], (3, NBX, NBY, BLOCK), jnp.float32) ** block_levels(keys[0], (3, NBX, NBY, BLOCK), ((1, 8), (2, 4)), -0.2, 0.2), 0.0, 1.0)
    dual_weight = draw_dual_weight(jax.random.fold_in(keys[5], 71), 0)
    target_mass = jnp.clip(0.2 + 0.6 * jax.random.uniform(keys[2], (NBX, NBY, BLOCK), jnp.float32) ** block_levels(keys[2], (NBX, NBY, BLOCK), ((0, 8), (1, 4)), -0.2, 0.2), 0.2, 0.8)
    block_list = draw_block_list(jax.random.fold_in(keys[5], 71), 0)
    block_count = draw_block_count(jax.random.fold_in(keys[5], 71), 0)
    return {"site_frac": site_frac, "dual_weight": dual_weight, "target_mass": target_mass, "block_list": block_list, "block_count": block_count}


entropy_scale = 0.5
step_rate = 0.5


def grid_points(first_row, how_many):
    serial = first_row + jnp.arange(how_many)
    cell_x = serial // (TY * Z)
    cell_y = (serial // Z) % TY
    cell_z = serial % Z
    return jnp.stack([cell_x, cell_y, cell_z]).astype(jnp.float32) + 0.5


def assign(points, chosen, usable, moments):
    spread = points[:, :, None] - chosen[:3, None, :]
    distance = spread[0] * spread[0] + spread[1] * spread[1] + spread[2] * spread[2]
    scores = jnp.where(usable[None, :], (chosen[3][None, :] - distance) / entropy_scale, -jnp.inf)
    peak_score = jnp.max(scores, axis=1, keepdims=True)
    weights = jnp.exp(scores - peak_score)
    shares = weights / jnp.sum(weights, axis=1, keepdims=True)
    masses = jnp.sum(shares, axis=0)
    if not moments:
        return masses, None, None
    moment = jnp.sum(shares[None] * spread, axis=1)
    offsets = -jnp.sum(shares[None] * spread, axis=2)
    return masses, moment, offsets


def wrapped(tile_pos, total_blocks):
    return (tile_pos * SB_SIDE - SB_SIDE + jnp.arange(3 * SB_SIDE)) % total_blocks


def tile_step(site_frac, duals, block_list, block_count, tile_id):
    tile_x = tile_id // N_GY
    tile_y = tile_id % N_GY
    row_ids = wrapped(tile_x, NBX)
    col_ids = wrapped(tile_y, NBY)
    fraction = site_frac[:, row_ids][:, :, col_ids]
    local_duals = duals[row_ids][:, col_ids]
    offset = (jnp.arange(3 * SB_SIDE) // SB_SIDE - 1).astype(jnp.float32)
    site_table = jnp.stack([fraction[0] * TX + offset[:, None, None] * TX,
                            fraction[1] * TY + offset[None, :, None] * TY,
                            fraction[2] * Z, local_duals])
    flat_table = site_table.reshape(4, 9 * SB_SIDE * SB_SIDE, BLOCK)
    chosen_ids = block_list[tile_x, tile_y]
    live_count = block_count[tile_x, tile_y]
    chosen = flat_table[:, chosen_ids].reshape(4, K_MAX * BLOCK)
    usable = jnp.arange(K_MAX * BLOCK) // BLOCK < live_count
    masses, moment, offsets = assign(grid_points(0, TX * TY * Z), chosen, usable, True)
    partials = jnp.concatenate([masses[None], moment], 0).reshape(4, K_MAX, BLOCK)
    partials = jnp.where((jnp.arange(K_MAX) < live_count)[None, :, None], partials, 0.0)
    summed = jnp.zeros((4, 9 * SB_SIDE * SB_SIDE, BLOCK), jnp.float32).at[:, chosen_ids].add(partials)
    return summed, offsets


def one_step(site_frac, duals, block_list, block_count):
    tile_total = N_GX * N_GY
    summed, offsets = lax.map(lambda tile_id: tile_step(site_frac, duals, block_list, block_count, tile_id),
                              jnp.arange(tile_total))
    tile_serial = jnp.arange(tile_total)
    row_ids = ((tile_serial // N_GY)[:, None] * SB_SIDE - SB_SIDE + jnp.arange(3 * SB_SIDE)[None, :]) % NBX
    col_ids = ((tile_serial % N_GY)[:, None] * SB_SIDE - SB_SIDE + jnp.arange(3 * SB_SIDE)[None, :]) % NBY
    pieces = summed.reshape(tile_total, 4, 3 * SB_SIDE, 3 * SB_SIDE, BLOCK).transpose(0, 2, 3, 1, 4)
    totals = jnp.zeros((NBX, NBY, 4, BLOCK), jnp.float32).at[row_ids[:, :, None], col_ids[:, None, :]].add(pieces)
    return totals.transpose(2, 0, 1, 3), offsets


def reference(site_frac, dual_weight, target_mass, block_list, block_count):
    totals, offsets = one_step(site_frac, dual_weight, block_list, block_count)
    dual_mid = dual_weight + step_rate * (target_mass - totals[0])
    totals, offsets = one_step(site_frac, dual_mid, block_list, block_count)
    new_dual = dual_mid + step_rate * (target_mass - totals[0])
    site_shift = totals[1:] / (totals[0] + target_mass)[None]
    displacement = offsets.reshape(N_GX, N_GY, 3, TX, TY, Z).transpose(2, 0, 3, 1, 4, 5).reshape(3, NX, NY, Z)
    return new_dual, site_shift, displacement
```

```python
import functools
import math

import jax
import jax.numpy as jnp
from jax import lax
from jax.experimental import pallas as pl
from jax.experimental.pallas import tpu as pltpu
from jax.sharding import PartitionSpec as P

TX = 4
TY = 4
Z = 256

entropy_scale = 0.5
step_rate = 0.5

SCALE = 1.0 / (entropy_scale * math.log(2.0))
DEAD = -1e30
LIFT = 40.0
HEAD = 2.0**30
UNIT_XY = 8.0
HALF_Z = 0.5 * Z
CHUNK = 16
AROUND = [d for d in range(9) if d != 4]
WIDE = [(a, b) for a in range(-2, 3) for b in range(-2, 3) if (a, b) != (0, 0)]
GROUPS = TX // 2
ROWS = 2 * TY
NT = (((1,), (1,)), ((), ()))
NN = (((1,), (0,)), ((), ()))


def halves(value):
    high = value.astype(jnp.bfloat16)
    return high, value - high.astype(jnp.float32)


def product(left, high, low, dims):
    return lax.dot_general(
        left, high, dims, preferred_element_type=jnp.float32
    ) + lax.dot_general(left, low, dims, preferred_element_type=jnp.float32)


def total_rows(value):
    for shift in (4, 2, 1):
        value = value + pltpu.roll(value, shift, 0)
    return value


def kernel(
    frac_ref, dual_ref, target_ref, list_ref, count_ref,
    new_ref, shift_ref, disp_ref,
    frac_all, dual_all, target_all, mid_all, part_send, part_recv, four_send, four_recv,
    list_held, count_held, table, base_ref, plain_ref, left_ref, g_high, g_low,
    wide_send, wide_recv, send_sem, recv_sem, local_sem,
):
    side = frac_ref.shape[1]
    block = frac_ref.shape[3]
    slots = list_ref.shape[2]
    columns = slots * block
    span = 3 * side
    gx, gy = lax.axis_index("gx"), lax.axis_index("gy")
    nx, ny = lax.axis_size("gx"), lax.axis_size("gy")

    def device(d):
        return (lax.rem(gx + d // 3 - 1 + nx, nx), lax.rem(gy + d % 3 - 1 + ny, ny))

    def far(a, b):
        return (lax.rem(gx + a + nx, nx), lax.rem(gy + b + ny, ny))

    def wide_copy(a, b):
        here = tuple(pl.ds(max(v, 0), 3 - abs(v)) for v in (a, b))
        there = tuple(pl.ds(max(-v, 0), 3 - abs(v)) for v in (a, b))
        e = (a + 2) * 5 + b + 2
        return pltpu.make_async_remote_copy(
            src_ref=part_send.at[here], dst_ref=part_recv.at[(24 - e,) + there],
            send_sem=wide_send.at[e], recv_sem=wide_recv.at[24 - e],
            device_id=far(a, b), device_id_type=pl.DeviceIdType.MESH,
        )

    def copy(phase, d, src, dst):
        return pltpu.make_async_remote_copy(
            src_ref=src, dst_ref=dst.at[8 - d],
            send_sem=send_sem.at[phase, d], recv_sem=recv_sem.at[phase, 8 - d],
            device_id=device(d), device_id_type=pl.DeviceIdType.MESH,
        )

    def begin(copies):
        for one in copies:
            one.start()
        return copies

    def finish(copies):
        for one in copies:
            one.wait()

    barrier = pltpu.get_barrier_semaphore()
    for a, b in WIDE:
        pl.semaphore_signal(
            barrier, inc=1, device_id=far(a, b), device_id_type=pl.DeviceIdType.MESH
        )
    finish(begin([
        pltpu.make_async_copy(src, dst, local_sem.at[n])
        for n, (src, dst) in enumerate([
            (frac_ref, frac_all.at[4]), (dual_ref, dual_all.at[4]), (target_ref, target_all.at[4]),
            (list_ref, list_held), (count_ref, count_held),
        ])
    ]))
    live = count_held[0, 0]
    places = []
    for m in range(slots):
        slot = list_held[0, 0, m]
        row, col = slot // span, slot % span
        places.append(((row // side) * 3 + col // side, row % side, col % side,
                       (row // side - 1).astype(jnp.float32) * TX,
                       (col // side - 1).astype(jnp.float32) * TY))
    pl.semaphore_wait(barrier, len(WIDE))

    first = begin([copy(0, d, frac_all.at[4], frac_all) for d in AROUND])
    first += begin([copy(1, d, dual_all.at[4], dual_all) for d in AROUND])
    goals = begin([copy(2, d, target_all.at[4], target_all) for d in AROUND])
    finish(first)

    for m in range(slots):
        tile, row, col, corner_x, corner_y = places[m]
        at = slice(m * block, (m + 1) * block)
        table[0:1, at] = frac_all[tile, 0, row, pl.ds(col, 1), :] * TX + corner_x
        table[1:2, at] = frac_all[tile, 1, row, pl.ds(col, 1), :] * TY + corner_y
        table[2:3, at] = frac_all[tile, 2, row, pl.ds(col, 1), :] * Z

    def load_duals(source):
        for m in range(slots):
            row = source[places[m][0], places[m][1], pl.ds(places[m][2], 1), :]
            table[3:4, m * block : (m + 1) * block] = jnp.where(m < live, row * SCALE, DEAD)

    load_duals(dual_all)

    serial = lax.broadcasted_iota(jnp.int32, (ROWS, columns), 0)
    step_x = (serial // TY).astype(jnp.float32) - 0.5
    step_y = (serial % TY).astype(jnp.float32) - 0.5 * (TY - 1)
    level_z = (lax.broadcasted_iota(jnp.int32, (ROWS, Z), 1).astype(jnp.float32) + 0.5 - HALF_Z) * (1.0 / HALF_Z)

    def centres(n):
        return (2 * n + 1.0) - table[0:1, :], 0.5 * TY - table[1:2, :]

    for n in range(GROUPS):
        centre_x, centre_y = centres(n)
        base_ref[n : n + 1, :] = -SCALE * (centre_x * centre_x + centre_y * centre_y)
        plain = jnp.exp2((-2.0 * SCALE) * (step_x * centre_x + step_y * centre_y))
        plain_ref[n] = plain
        high, low = halves(plain)
        high = high.astype(jnp.float32)
        low = low.astype(jnp.bfloat16).astype(jnp.float32)
        left_ref[n, 0:16] = jnp.concatenate([high, low], axis=0).astype(jnp.bfloat16)

    def extend():
        for n in range(GROUPS):
            centre_x, centre_y = centres(n)
            plain = plain_ref[n]
            high, low = halves(plain)
            kept = high.astype(jnp.float32) + low.astype(jnp.bfloat16).astype(jnp.float32)
            deep = kept * ((table[2:3, :] - HALF_Z) * (1.0 / HALF_Z))
            first = deep.astype(jnp.bfloat16).astype(jnp.float32)
            second = (deep - first).astype(jnp.bfloat16).astype(jnp.float32)
            third = deep - first - second
            across = plain * ((centre_x + step_x) * (1.0 / UNIT_XY))
            aside = plain * ((centre_y + step_y) * (1.0 / UNIT_XY))
            flat = jnp.concatenate([across, aside], axis=0)
            high, low = halves(flat)
            left_ref[n, 16:32] = jnp.concatenate([first, second], axis=0).astype(jnp.bfloat16)
            left_ref[n, 32:48] = jnp.concatenate([third, jnp.zeros_like(third)], axis=0).astype(jnp.bfloat16)
            left_ref[n, 48:64] = high
            left_ref[n, 64:80] = low.astype(jnp.bfloat16)

    steps = lax.broadcasted_iota(jnp.int32, (CHUNK, columns), 0).astype(jnp.float32) - (0.5 * CHUNK - 0.5)

    def build():
        levels = [base_ref[n : n + 1, :] + table[3:4, :] for n in range(GROUPS)]

        def chunk(c, carry):
            start = pl.multiple_of(c * CHUNK, CHUNK)
            away = table[2:3, :] - (start.astype(jnp.float32) + 0.5 * CHUNK)
            curve = away * away * (-SCALE)
            lean = steps * (away * (2.0 * SCALE))
            for n in range(GROUPS):
                score = lean + (levels[n] + curve)
                g = jnp.exp2(score - (jnp.max(score, axis=1, keepdims=True) - LIFT))
                high, low = halves(g)
                g_high[n, pl.ds(start, CHUNK), :] = high
                g_low[n, pl.ds(start, CHUNK), :] = low.astype(jnp.bfloat16)
            return carry

        lax.fori_loop(0, Z // CHUNK, chunk, 0, unroll=2)

    build()
    pairs = []
    for n in range(GROUPS):
        found = product(left_ref[n, 0:16], g_high[n], g_low[n], NT)
        inverse = HEAD / (found[0:8] + found[8:16])
        high, low = halves(inverse)
        pairs.append(jnp.concatenate([high.astype(jnp.float32), low], axis=0).astype(jnp.bfloat16))
    total = jnp.zeros((ROWS, columns), jnp.float32)
    for n in range(GROUPS):
        found = product(pairs[n], g_high[n], g_low[n], NN)
        total = total + plain_ref[n] * (found[0:8] + found[8:16])
    rows = total_rows(total) * (1.0 / HEAD)
    shape = (side, side, block)
    inner = lax.broadcasted_iota(jnp.int32, shape, 0) * side + lax.broadcasted_iota(
        jnp.int32, shape, 1
    )
    wanted = [places[m][1] * side + places[m][2] + (side * side) * places[m][0] for m in range(slots)]
    spread = [
        jnp.broadcast_to(rows[0:1, m * block : (m + 1) * block][None], shape) for m in range(slots)
    ]
    for d in range(9):
        found = jnp.zeros(shape, jnp.float32)
        for m in range(slots):
            found = found + jnp.where(inner == wanted[m] - side * side * d, spread[m], 0.0)
        part_send[d // 3, d % 3] = found
    second = begin([wide_copy(a, b) for a, b in WIDE])
    extend()
    finish(goals)
    finish(second)
    for i in range(3):
        for j in range(3):
            mass = part_send[i, j]
            for a, b in WIDE:
                if 0 <= i - max(a, 0) < 3 - abs(a) and 0 <= j - max(b, 0) < 3 - abs(b):
                    mass = mass + part_recv[(a + 2) * 5 + b + 2, i, j]
            d = 3 * i + j
            mid_all[d] = dual_all[d] + step_rate * (target_all[d] - mass)

    load_duals(mid_all)
    build()
    pairs = []
    for n in range(GROUPS):
        found = product(left_ref[n], g_high[n], g_low[n], NT)
        inverse = HEAD / (found[0:8] + found[8:16])
        high, low = halves(inverse)
        high = high.astype(jnp.float32)
        low = low.astype(jnp.bfloat16).astype(jnp.float32)
        deep = (high + low) * level_z
        first = deep.astype(jnp.bfloat16).astype(jnp.float32)
        second = (deep - first).astype(jnp.bfloat16).astype(jnp.float32)
        third = deep - first - second
        pairs.append(jnp.concatenate(
            [high, low, first, second, third, jnp.zeros_like(third)], axis=0
        ).astype(jnp.bfloat16))
        inverse = inverse * (1.0 / HEAD)
        offsets = (
            (found[48:56] + found[64:72]) * inverse * -UNIT_XY,
            (found[56:64] + found[72:80]) * inverse * -UNIT_XY,
            ((found[16:24] + found[24:32] + found[32:40]) * inverse - level_z) * HALF_Z,
        )
        for c in range(3):
            for r in range(2):
                disp_ref[c, 2 * n + r] = offsets[c][TY * r : TY * r + TY]
    sums = [jnp.zeros((ROWS, columns), jnp.float32) for _ in range(4)]
    for n in range(GROUPS):
        centre_x, centre_y = centres(n)
        found = product(pairs[n], g_high[n], g_low[n], NN)
        plain = plain_ref[n]
        mass = plain * (found[0:8] + found[8:16])
        deep = plain * (found[16:24] + found[24:32] + found[32:40])
        sums[0] = sums[0] + mass
        sums[1] = sums[1] + mass * (centre_x + step_x)
        sums[2] = sums[2] + mass * (centre_y + step_y)
        sums[3] = sums[3] + (deep * HALF_Z - mass * (table[2:3, :] - HALF_Z))
    sums = [total_rows(v) for v in sums]
    kind = serial % 4
    rows = jnp.where(
        kind < 2, jnp.where(kind == 0, sums[0], sums[1]), jnp.where(kind == 2, sums[2], sums[3])
    ) * (1.0 / HEAD)
    half = lax.broadcasted_iota(jnp.int32, (8, block), 0) // 4
    for d in range(9):
        for v in range(side * side // 2):
            found = jnp.zeros((8, block), jnp.float32)
            for m in range(slots):
                here = half == wanted[m] - (side * side * d + 2 * v)
                found = found + jnp.where(here, rows[:, m * block : (m + 1) * block], 0.0)
            four_send[d, 8 * v : 8 * v + 8, :] = found
    fourth = begin([copy(3, d, four_send.at[d], four_recv) for d in AROUND])
    finish(fourth)
    four = four_send[4]
    for d in AROUND:
        four = four + four_recv[d]
    for i in range(side * side):
        r, c = i // side, i % side
        goal = target_all[4, r, c : c + 1, :]
        found = four[4 * i : 4 * i + 1]
        new_ref[r, c : c + 1, :] = mid_all[4, r, c : c + 1, :] + step_rate * (goal - found)
        weight = 1.0 / (found + goal)
        for k in range(3):
            shift_ref[k, r, c : c + 1, :] = four[4 * i + k + 1 : 4 * i + k + 2] * weight


def place_results(new_ref, shift_ref, disp_ref, new_out, shift_out, disp_out, sems):
    pairs = ((disp_ref, disp_out), (shift_ref, shift_out), (new_ref, new_out))
    copies = [pltpu.make_async_copy(src, dst, sems.at[n]) for n, (src, dst) in enumerate(pairs)]
    for one in copies:
        one.start()
    for one in copies:
        one.wait()


def on_device(site_frac, dual_weight, target_mass, block_list, block_count):
    side = site_frac.shape[1]
    block = site_frac.shape[3]
    columns = block_list.shape[2] * block
    f32, bf16, i32 = jnp.float32, jnp.bfloat16, jnp.int32
    vmem = pl.BlockSpec(memory_space=pltpu.VMEM)
    place = pl.BlockSpec(memory_space=pl.ANY)
    results = pl.pallas_call(
        kernel,
        out_shape=(
            pltpu.VMEM(dual_weight.shape, f32),
            pltpu.VMEM(site_frac.shape, f32),
            pltpu.VMEM((3, TX, TY, Z), f32),
        ),
        in_specs=[place] * 5,
        out_specs=(vmem, vmem, vmem),
        scratch_shapes=[
            pltpu.VMEM((9,) + site_frac.shape, f32),
            pltpu.VMEM((9,) + dual_weight.shape, f32),
            pltpu.VMEM((9,) + target_mass.shape, f32),
            pltpu.VMEM((9,) + dual_weight.shape, f32),
            pltpu.VMEM((3, 3, side, side, block), f32),
            pltpu.VMEM((25, 3, 3, side, side, block), f32),
            pltpu.VMEM((9, 4 * side * side, block), f32),
            pltpu.VMEM((9, 4 * side * side, block), f32),
            pltpu.SMEM(block_list.shape, i32),
            pltpu.SMEM(block_count.shape, i32),
            pltpu.VMEM((8, columns), f32),
            pltpu.VMEM((8, columns), f32),
            pltpu.VMEM((GROUPS, ROWS, columns), f32),
            pltpu.VMEM((GROUPS, 10 * ROWS, columns), bf16),
            pltpu.VMEM((GROUPS, Z, columns), bf16),
            pltpu.VMEM((GROUPS, Z, columns), bf16),
            pltpu.SemaphoreType.DMA((25,)),
            pltpu.SemaphoreType.DMA((25,)),
            pltpu.SemaphoreType.DMA((4, 9)),
            pltpu.SemaphoreType.DMA((4, 9)),
            pltpu.SemaphoreType.DMA((5,)),
        ],
        compiler_params=pltpu.CompilerParams(collective_id=0, has_side_effects=True),
        name="transport",
    )(site_frac, dual_weight, target_mass, block_list, block_count)
    return pl.pallas_call(
        place_results,
        out_shape=tuple(jax.ShapeDtypeStruct(r.shape, f32) for r in results),
        in_specs=[vmem] * 3,
        out_specs=(pl.BlockSpec(memory_space=pltpu.HBM),) * 3,
        scratch_shapes=[pltpu.SemaphoreType.DMA((3,))],
        name="place",
    )(*[pltpu.with_memory_space_constraint(r, pltpu.VMEM) for r in results])


def solution(mesh):
    in_specs = (
        P(None, "gx", "gy", None),
        P("gx", "gy", None),
        P("gx", "gy", None),
        P("gx", "gy", None),
        P("gx", "gy"),
    )
    out_specs = (P("gx", "gy", None), P(None, "gx", "gy", None), P(None, "gx", "gy", None))
    return jax.shard_map(
        on_device, mesh=mesh, in_specs=in_specs, out_specs=out_specs, check_vma=False
    )
```

```python
import functools
import math

import jax
import jax.numpy as jnp
from jax import lax
from jax.experimental import pallas as pl
from jax.experimental.pallas import tpu as pltpu
from jax.sharding import PartitionSpec as P

TX = 4
TY = 4
Z = 256

entropy_scale = 0.5
step_rate = 0.5

SCALE = 1.0 / (entropy_scale * math.log(2.0))
DEAD = -1e30
LIFT = 40.0
HEAD = 2.0**30
UNIT_XY = 8.0
HALF_Z = 0.5 * Z
CHUNK = 16
WIDE = [(a, b) for a in range(-2, 3) for b in range(-2, 3) if (a, b) != (0, 0)]
GROUPS = TX // 2
ROWS = 2 * TY
NT = (((1,), (1,)), ((), ()))
NN = (((1,), (0,)), ((), ()))


def halves(value):
    high = value.astype(jnp.bfloat16)
    return high, value - high.astype(jnp.float32)


def product(left, high, low, dims):
    return lax.dot_general(
        left, high, dims, preferred_element_type=jnp.float32
    ) + lax.dot_general(left, low, dims, preferred_element_type=jnp.float32)


def total_rows(value):
    for shift in (4, 2, 1):
        value = value + pltpu.roll(value, shift, 0)
    return value


def kernel(
    frac_ref, dual_ref, target_ref, list_ref, count_ref,
    new_ref, shift_ref, disp_ref,
    mine, halo, mid_all, part_send, part_recv, four_send, four_recv, disp_send, mid_home,
    list_mine, count_mine, list_held, count_held,
    table, base_ref, plain_ref, left_ref, g_high, g_low,
    wide_send, wide_recv, send_sem, recv_sem, home_send, home_recv, local_sem,
):
    side = frac_ref.shape[1]
    block = frac_ref.shape[3]
    slots = list_ref.shape[2]
    columns = slots * block
    span = 3 * side
    gx, gy = lax.axis_index("gx"), lax.axis_index("gy")
    nx, ny = lax.axis_size("gx"), lax.axis_size("gy")

    half = max(nx // 2, 1)
    rest = nx - half

    def wrap(t):
        return lax.rem(t + nx, nx)

    def worker(t):
        return jnp.where(t < half, lax.rem(t + half - 1, half), half + lax.rem(t - half + nx + 1, rest))

    tile = jnp.where(gx < half, lax.rem(gx + 1, half), half + lax.rem(gx - half + rest - 1 + nx * rest, rest))

    def column(b):
        return lax.rem(gy + b + ny, ny)

    def far(a, b):
        return (worker(wrap(tile + a)), column(b))

    def wide_copy(a, b):
        here = tuple(pl.ds(max(v, 0), 3 - abs(v)) for v in (a, b))
        there = tuple(pl.ds(max(-v, 0), 3 - abs(v)) for v in (a, b))
        e = (a + 2) * 5 + b + 2
        return pltpu.make_async_remote_copy(
            src_ref=part_send.at[here], dst_ref=part_recv.at[(24 - e,) + there],
            send_sem=wide_send.at[e], recv_sem=wide_recv.at[24 - e],
            device_id=far(a, b), device_id_type=pl.DeviceIdType.MESH,
        )

    class Spread:
        def __init__(self, phase, d, where, src, dst):
            self.near = d % 3 == 1 and d != 4
            self.own = where == gx
            self.remote = pltpu.make_async_remote_copy(
                src_ref=src, dst_ref=dst.at[8 - d],
                send_sem=send_sem.at[phase, d], recv_sem=recv_sem.at[phase, 8 - d],
                device_id=(where, column(d % 3 - 1)), device_id_type=pl.DeviceIdType.MESH,
            )
            if self.near:
                self.local = pltpu.make_async_copy(src, dst.at[8 - d], recv_sem.at[phase, 8 - d])

        def start(self):
            if not self.near:
                self.remote.start()
                return
            pl.when(self.own)(self.local.start)
            pl.when(jnp.logical_not(self.own))(self.remote.start)

        def wait(self):
            self.remote.wait_recv()

        def wait_send(self):
            if not self.near:
                self.remote.wait_send()
                return
            pl.when(jnp.logical_not(self.own))(self.remote.wait_send)

    def home_copy(n, src, dst):
        return pltpu.make_async_remote_copy(
            src_ref=src, dst_ref=dst, send_sem=home_send.at[n], recv_sem=home_recv.at[n],
            device_id=(tile, gy), device_id_type=pl.DeviceIdType.MESH,
        )

    def begin(copies):
        for one in copies:
            one.start()
        return copies

    def finish(copies):
        for one in copies:
            one.wait()

    barrier = pltpu.get_barrier_semaphore()
    for a in range(-1, 2):
        for b in range(-1, 2):
            pl.semaphore_signal(
                barrier, inc=1, device_id=(wrap(tile + a), column(b)),
                device_id_type=pl.DeviceIdType.MESH,
            )
    finish(begin([
        pltpu.make_async_copy(src, dst, local_sem.at[n])
        for n, (src, dst) in enumerate([
            (frac_ref, mine.at[0:3]), (dual_ref, mine.at[3]), (target_ref, mine.at[4]),
            (list_ref, list_mine), (count_ref, count_mine),
        ])
    ]))
    pl.semaphore_wait(barrier, 9)

    listed = begin([
        pltpu.make_async_remote_copy(
            src_ref=src, dst_ref=dst, send_sem=home_send.at[n], recv_sem=home_recv.at[n],
            device_id=(worker(gx), gy), device_id_type=pl.DeviceIdType.MESH,
        )
        for n, src, dst in ((0, list_mine, list_held), (1, count_mine, count_held))
    ])
    opening = begin([
        Spread(0, d, worker(wrap(gx + d // 3 - 1)), mine, halo) for d in range(9)
    ])
    finish(listed)
    live = count_held[0, 0]
    places = []
    for m in range(slots):
        slot = list_held[0, 0, m]
        row, col = slot // span, slot % span
        places.append(((row // side) * 3 + col // side, row % side, col % side,
                       (row // side - 1).astype(jnp.float32) * TX,
                       (col // side - 1).astype(jnp.float32) * TY))
    finish(opening)

    for m in range(slots):
        block_tile, row, col, corner_x, corner_y = places[m]
        at = slice(m * block, (m + 1) * block)
        table[0:1, at] = halo[block_tile, 0, row, pl.ds(col, 1), :] * TX + corner_x
        table[1:2, at] = halo[block_tile, 1, row, pl.ds(col, 1), :] * TY + corner_y
        table[2:3, at] = halo[block_tile, 2, row, pl.ds(col, 1), :] * Z

    def load_duals(source):
        for m in range(slots):
            row = source(places[m][0], places[m][1], pl.ds(places[m][2], 1))
            table[3:4, m * block : (m + 1) * block] = jnp.where(m < live, row * SCALE, DEAD)

    load_duals(lambda d, r, c: halo[d, 3, r, c, :])

    serial = lax.broadcasted_iota(jnp.int32, (ROWS, columns), 0)
    step_x = (serial // TY).astype(jnp.float32) - 0.5
    step_y = (serial % TY).astype(jnp.float32) - 0.5 * (TY - 1)
    level_z = (lax.broadcasted_iota(jnp.int32, (ROWS, Z), 1).astype(jnp.float32) + 0.5 - HALF_Z) * (1.0 / HALF_Z)

    def centres(n):
        return (2 * n + 1.0) - table[0:1, :], 0.5 * TY - table[1:2, :]

    for n in range(GROUPS):
        centre_x, centre_y = centres(n)
        base_ref[n : n + 1, :] = -SCALE * (centre_x * centre_x + centre_y * centre_y)
        plain = jnp.exp2((-2.0 * SCALE) * (step_x * centre_x + step_y * centre_y))
        plain_ref[n] = plain
        high, low = halves(plain)
        high = high.astype(jnp.float32)
        low = low.astype(jnp.bfloat16).astype(jnp.float32)
        left_ref[n, 0:16] = jnp.concatenate([high, low], axis=0).astype(jnp.bfloat16)

    def extend():
        for n in range(GROUPS):
            centre_x, centre_y = centres(n)
            plain = plain_ref[n]
            high, low = halves(plain)
            kept = high.astype(jnp.float32) + low.astype(jnp.bfloat16).astype(jnp.float32)
            deep = kept * ((table[2:3, :] - HALF_Z) * (1.0 / HALF_Z))
            first = deep.astype(jnp.bfloat16).astype(jnp.float32)
            second = (deep - first).astype(jnp.bfloat16).astype(jnp.float32)
            third = deep - first - second
            across = plain * ((centre_x + step_x) * (1.0 / UNIT_XY))
            aside = plain * ((centre_y + step_y) * (1.0 / UNIT_XY))
            flat = jnp.concatenate([across, aside], axis=0)
            high, low = halves(flat)
            left_ref[n, 16:32] = jnp.concatenate([first, second], axis=0).astype(jnp.bfloat16)
            left_ref[n, 32:48] = jnp.concatenate([third, jnp.zeros_like(third)], axis=0).astype(jnp.bfloat16)
            left_ref[n, 48:64] = high
            left_ref[n, 64:80] = low.astype(jnp.bfloat16)

    steps = lax.broadcasted_iota(jnp.int32, (CHUNK, columns), 0).astype(jnp.float32) - (0.5 * CHUNK - 0.5)

    def build():
        levels = [base_ref[n : n + 1, :] + table[3:4, :] for n in range(GROUPS)]

        def chunk(c, carry):
            start = pl.multiple_of(c * CHUNK, CHUNK)
            away = table[2:3, :] - (start.astype(jnp.float32) + 0.5 * CHUNK)
            curve = away * away * (-SCALE)
            lean = steps * (away * (2.0 * SCALE))
            for n in range(GROUPS):
                score = lean + (levels[n] + curve)
                g = jnp.exp2(score - (jnp.max(score, axis=1, keepdims=True) - LIFT))
                high, low = halves(g)
                g_high[n, pl.ds(start, CHUNK), :] = high
                g_low[n, pl.ds(start, CHUNK), :] = low.astype(jnp.bfloat16)
            return carry

        lax.fori_loop(0, Z // CHUNK, chunk, 0, unroll=2)

    build()
    pairs = []
    for n in range(GROUPS):
        found = product(left_ref[n, 0:16], g_high[n], g_low[n], NT)
        inverse = HEAD / (found[0:8] + found[8:16])
        high, low = halves(inverse)
        pairs.append(jnp.concatenate([high.astype(jnp.float32), low], axis=0).astype(jnp.bfloat16))
    total = jnp.zeros((ROWS, columns), jnp.float32)
    for n in range(GROUPS):
        found = product(pairs[n], g_high[n], g_low[n], NN)
        total = total + plain_ref[n] * (found[0:8] + found[8:16])
    rows = total_rows(total) * (1.0 / HEAD)
    shape = (side, side, block)
    inner = lax.broadcasted_iota(jnp.int32, shape, 0) * side + lax.broadcasted_iota(
        jnp.int32, shape, 1
    )
    wanted = [places[m][1] * side + places[m][2] + (side * side) * places[m][0] for m in range(slots)]
    spread = [
        jnp.broadcast_to(rows[0:1, m * block : (m + 1) * block][None], shape) for m in range(slots)
    ]
    for d in range(9):
        found = jnp.zeros(shape, jnp.float32)
        for m in range(slots):
            found = found + jnp.where(inner == wanted[m] - side * side * d, spread[m], 0.0)
        part_send[d // 3, d % 3] = found
    second = begin([wide_copy(a, b) for a, b in WIDE])
    extend()
    finish(second)
    for i in range(3):
        for j in range(3):
            mass = part_send[i, j]
            for a, b in WIDE:
                if 0 <= i - max(a, 0) < 3 - abs(a) and 0 <= j - max(b, 0) < 3 - abs(b):
                    mass = mass + part_recv[(a + 2) * 5 + b + 2, i, j]
            d = 3 * i + j
            mid_all[d] = halo[d, 3] + step_rate * (halo[d, 4] - mass)

    homeward = begin([home_copy(2, mid_all.at[4], mid_home)])
    load_duals(lambda d, r, c: mid_all[d, r, c, :])
    build()
    pairs = []
    for n in range(GROUPS):
        found = product(left_ref[n], g_high[n], g_low[n], NT)
        inverse = HEAD / (found[0:8] + found[8:16])
        high, low = halves(inverse)
        high = high.astype(jnp.float32)
        low = low.astype(jnp.bfloat16).astype(jnp.float32)
        deep = (high + low) * level_z
        first = deep.astype(jnp.bfloat16).astype(jnp.float32)
        second = (deep - first).astype(jnp.bfloat16).astype(jnp.float32)
        third = deep - first - second
        pairs.append(jnp.concatenate(
            [high, low, first, second, third, jnp.zeros_like(third)], axis=0
        ).astype(jnp.bfloat16))
        inverse = inverse * (1.0 / HEAD)
        offsets = (
            (found[48:56] + found[64:72]) * inverse * -UNIT_XY,
            (found[56:64] + found[72:80]) * inverse * -UNIT_XY,
            ((found[16:24] + found[24:32] + found[32:40]) * inverse - level_z) * HALF_Z,
        )
        for c in range(3):
            for r in range(2):
                disp_send[c, 2 * n + r] = offsets[c][TY * r : TY * r + TY]
        part = (slice(None), pl.ds(2 * n, 2))
        homeward += begin([home_copy(3 + n, disp_send.at[part], disp_ref.at[part])])
    sums = [jnp.zeros((ROWS, columns), jnp.float32) for _ in range(4)]
    for n in range(GROUPS):
        centre_x, centre_y = centres(n)
        found = product(pairs[n], g_high[n], g_low[n], NN)
        plain = plain_ref[n]
        mass = plain * (found[0:8] + found[8:16])
        deep = plain * (found[16:24] + found[24:32] + found[32:40])
        sums[0] = sums[0] + mass
        sums[1] = sums[1] + mass * (centre_x + step_x)
        sums[2] = sums[2] + mass * (centre_y + step_y)
        sums[3] = sums[3] + (deep * HALF_Z - mass * (table[2:3, :] - HALF_Z))
    sums = [total_rows(v) for v in sums]
    kind = serial % 4
    rows = jnp.where(
        kind < 2, jnp.where(kind == 0, sums[0], sums[1]), jnp.where(kind == 2, sums[2], sums[3])
    ) * (1.0 / HEAD)
    upper = lax.broadcasted_iota(jnp.int32, (8, block), 0) // 4
    for d in range(9):
        for v in range(side * side // 2):
            found = jnp.zeros((8, block), jnp.float32)
            for m in range(slots):
                here = upper == wanted[m] - (side * side * d + 2 * v)
                found = found + jnp.where(here, rows[:, m * block : (m + 1) * block], 0.0)
            four_send[d, 8 * v : 8 * v + 8, :] = found
    closing = begin([
        Spread(1, d, wrap(tile + d // 3 - 1), four_send.at[d], four_recv) for d in range(9)
    ])
    finish(closing)
    four = four_recv[0]
    for d in range(1, 9):
        four = four + four_recv[d]
    homeward[0].wait()
    for i in range(side * side):
        r, c = i // side, i % side
        goal = mine[4, r, c : c + 1, :]
        found = four[4 * i : 4 * i + 1]
        new_ref[r, c : c + 1, :] = mid_home[r, c : c + 1, :] + step_rate * (goal - found)
        weight = 1.0 / (found + goal)
        for k in range(3):
            shift_ref[k, r, c : c + 1, :] = four[4 * i + k + 1 : 4 * i + k + 2] * weight
    finish(homeward[1:])
    for one in opening + closing:
        one.wait_send()


def place_results(new_ref, shift_ref, disp_ref, new_out, shift_out, disp_out, sems):
    pairs = ((disp_ref, disp_out), (shift_ref, shift_out), (new_ref, new_out))
    copies = [pltpu.make_async_copy(src, dst, sems.at[n]) for n, (src, dst) in enumerate(pairs)]
    for one in copies:
        one.start()
    for one in copies:
        one.wait()


def on_device(site_frac, dual_weight, target_mass, block_list, block_count):
    side = site_frac.shape[1]
    block = site_frac.shape[3]
    columns = block_list.shape[2] * block
    f32, bf16, i32 = jnp.float32, jnp.bfloat16, jnp.int32
    vmem = pl.BlockSpec(memory_space=pltpu.VMEM)
    place = pl.BlockSpec(memory_space=pl.ANY)
    results = pl.pallas_call(
        kernel,
        out_shape=(
            pltpu.VMEM(dual_weight.shape, f32),
            pltpu.VMEM(site_frac.shape, f32),
            pltpu.VMEM((3, TX, TY, Z), f32),
        ),
        in_specs=[place] * 5,
        out_specs=(vmem, vmem, vmem),
        scratch_shapes=[
            pltpu.VMEM((5,) + dual_weight.shape, f32),
            pltpu.VMEM((9, 5) + dual_weight.shape, f32),
            pltpu.VMEM((9,) + dual_weight.shape, f32),
            pltpu.VMEM((3, 3, side, side, block), f32),
            pltpu.VMEM((25, 3, 3, side, side, block), f32),
            pltpu.VMEM((9, 4 * side * side, block), f32),
            pltpu.VMEM((9, 4 * side * side, block), f32),
            pltpu.VMEM((3, TX, TY, Z), f32),
            pltpu.VMEM(dual_weight.shape, f32),
            pltpu.SMEM(block_list.shape, i32),
            pltpu.SMEM(block_count.shape, i32),
            pltpu.SMEM(block_list.shape, i32),
            pltpu.SMEM(block_count.shape, i32),
            pltpu.VMEM((8, columns), f32),
            pltpu.VMEM((8, columns), f32),
            pltpu.VMEM((GROUPS, ROWS, columns), f32),
            pltpu.VMEM((GROUPS, 10 * ROWS, columns), bf16),
            pltpu.VMEM((GROUPS, Z, columns), bf16),
            pltpu.VMEM((GROUPS, Z, columns), bf16),
            pltpu.SemaphoreType.DMA((25,)),
            pltpu.SemaphoreType.DMA((25,)),
            pltpu.SemaphoreType.DMA((2, 9)),
            pltpu.SemaphoreType.DMA((2, 9)),
            pltpu.SemaphoreType.DMA((3 + GROUPS,)),
            pltpu.SemaphoreType.DMA((3 + GROUPS,)),
            pltpu.SemaphoreType.DMA((5,)),
        ],
        compiler_params=pltpu.CompilerParams(collective_id=0, has_side_effects=True),
        name="transport",
    )(site_frac, dual_weight, target_mass, block_list, block_count)
    return pl.pallas_call(
        place_results,
        out_shape=tuple(jax.ShapeDtypeStruct(r.shape, f32) for r in results),
        in_specs=[vmem] * 3,
        out_specs=(pl.BlockSpec(memory_space=pltpu.HBM),) * 3,
        scratch_shapes=[pltpu.SemaphoreType.DMA((3,))],
        name="place",
    )(*[pltpu.with_memory_space_constraint(r, pltpu.VMEM) for r in results])


def solution(mesh):
    in_specs = (
        P(None, "gx", "gy", None),
        P("gx", "gy", None),
        P("gx", "gy", None),
        P("gx", "gy", None),
        P("gx", "gy"),
    )
    out_specs = (P("gx", "gy", None), P(None, "gx", "gy", None), P(None, "gx", "gy", None))
    return jax.shard_map(
        on_device, mesh=mesh, in_specs=in_specs, out_specs=out_specs, check_vma=False
    )
```

```python
import functools
import math

import jax
import jax.numpy as jnp
from jax import lax
from jax.experimental import pallas as pl
from jax.experimental.pallas import tpu as pltpu
from jax.sharding import PartitionSpec as P

TX = 4
TY = 4
Z = 256

entropy_scale = 0.5
step_rate = 0.5

SCALE = 1.0 / (entropy_scale * math.log(2.0))
DEAD = -1e30
LIFT = 40.0
HEAD = 2.0**30
UNIT_XY = 8.0
HALF_Z = 0.5 * Z
CHUNK = 32
WIDE = sorted([(a, b) for a in range(-2, 3) for b in range(-2, 3) if (a, b) != (0, 0)], key=lambda v: -abs(v[0]) * 3 - abs(v[1]))
GROUPS = TX // 2
ROWS = 2 * TY
NT = (((1,), (1,)), ((), ()))
NN = (((1,), (0,)), ((), ()))


def halves(value):
    high = value.astype(jnp.bfloat16)
    return high, value - high.astype(jnp.float32)


def product(left, high, low, dims):
    return lax.dot_general(
        left, high, dims, preferred_element_type=jnp.float32
    ) + lax.dot_general(left, low, dims, preferred_element_type=jnp.float32)


def total_rows(value):
    for shift in (4, 2, 1):
        value = value + pltpu.roll(value, shift, 0)
    return value


def kernel(
    frac_ref, dual_ref, target_ref, list_ref, count_ref,
    new_ref, shift_ref, disp_ref,
    mine, halo, mid_all, part_send, part_recv, four_send, four_recv, disp_send, mid_home,
    list_mine, count_mine, list_held, count_held,
    table, base_ref, plain_ref, left_ref, shape_ref, g_high, g_low,
    wide_send, wide_recv, send_sem, recv_sem, home_send, home_recv, local_sem,
):
    side = frac_ref.shape[1]
    block = frac_ref.shape[3]
    slots = list_ref.shape[2]
    columns = slots * block
    span = 3 * side
    gx, gy = lax.axis_index("gx"), lax.axis_index("gy")
    nx, ny = lax.axis_size("gx"), lax.axis_size("gy")

    half = max(nx // 2, 1)
    rest = nx - half

    def wrap(t):
        return lax.rem(t + nx, nx)

    def worker(t):
        return jnp.where(t < half, lax.rem(t + half - 1, half), half + lax.rem(t - half + nx + 1, rest))

    tile = jnp.where(gx < half, lax.rem(gx + 1, half), half + lax.rem(gx - half + rest - 1 + nx * rest, rest))

    def column(b):
        return lax.rem(gy + b + ny, ny)

    def far(a, b):
        return (worker(wrap(tile + a)), column(b))

    def wide_copy(a, b):
        here = tuple(pl.ds(max(v, 0), 3 - abs(v)) for v in (a, b))
        there = tuple(pl.ds(max(-v, 0), 3 - abs(v)) for v in (a, b))
        e = (a + 2) * 5 + b + 2
        return pltpu.make_async_remote_copy(
            src_ref=part_send.at[here], dst_ref=part_recv.at[(24 - e,) + there],
            send_sem=wide_send.at[e], recv_sem=wide_recv.at[24 - e],
            device_id=far(a, b), device_id_type=pl.DeviceIdType.MESH,
        )

    class Spread:
        def __init__(self, phase, d, where, src, dst):
            self.near = d % 3 == 1 and d != 4
            self.own = where == gx
            self.remote = pltpu.make_async_remote_copy(
                src_ref=src, dst_ref=dst.at[8 - d],
                send_sem=send_sem.at[phase, d], recv_sem=recv_sem.at[phase, 8 - d],
                device_id=(where, column(d % 3 - 1)), device_id_type=pl.DeviceIdType.MESH,
            )
            if self.near:
                self.local = pltpu.make_async_copy(src, dst.at[8 - d], recv_sem.at[phase, 8 - d])

        def start(self):
            if not self.near:
                self.remote.start()
                return
            pl.when(self.own)(self.local.start)
            pl.when(jnp.logical_not(self.own))(self.remote.start)

        def wait(self):
            self.remote.wait_recv()

        def wait_send(self):
            if not self.near:
                self.remote.wait_send()
                return
            pl.when(jnp.logical_not(self.own))(self.remote.wait_send)

    def home_copy(n, src, dst):
        return pltpu.make_async_remote_copy(
            src_ref=src, dst_ref=dst, send_sem=home_send.at[n], recv_sem=home_recv.at[n],
            device_id=(tile, gy), device_id_type=pl.DeviceIdType.MESH,
        )

    def begin(copies):
        for one in copies:
            one.start()
        return copies

    def finish(copies):
        for one in copies:
            one.wait()

    barrier = pltpu.get_barrier_semaphore()
    for a in range(-1, 2):
        for b in range(-1, 2):
            pl.semaphore_signal(
                barrier, inc=1, device_id=(wrap(tile + a), column(b)),
                device_id_type=pl.DeviceIdType.MESH,
            )
    finish(begin([
        pltpu.make_async_copy(src, dst, local_sem.at[n])
        for n, (src, dst) in enumerate([
            (frac_ref, mine.at[0:3]), (dual_ref, mine.at[3]), (target_ref, mine.at[4]),
            (list_ref, list_mine), (count_ref, count_mine),
        ])
    ]))
    pl.semaphore_wait(barrier, 9)

    listed = begin([
        pltpu.make_async_remote_copy(
            src_ref=src, dst_ref=dst, send_sem=home_send.at[n], recv_sem=home_recv.at[n],
            device_id=(worker(gx), gy), device_id_type=pl.DeviceIdType.MESH,
        )
        for n, src, dst in ((0, list_mine, list_held), (1, count_mine, count_held))
    ])
    opening = begin([
        Spread(0, d, worker(wrap(gx + d // 3 - 1)), mine, halo) for d in range(9)
    ])
    finish(listed)
    live = count_held[0, 0]
    places = []
    for m in range(slots):
        slot = list_held[0, 0, m]
        row, col = slot // span, slot % span
        places.append(((row // side) * 3 + col // side, row % side, col % side,
                       (row // side - 1).astype(jnp.float32) * TX,
                       (col // side - 1).astype(jnp.float32) * TY))
    finish(opening)

    for m in range(slots):
        block_tile, row, col, corner_x, corner_y = places[m]
        at = slice(m * block, (m + 1) * block)
        table[0:1, at] = halo[block_tile, 0, row, pl.ds(col, 1), :] * TX + corner_x
        table[1:2, at] = halo[block_tile, 1, row, pl.ds(col, 1), :] * TY + corner_y
        table[2:3, at] = halo[block_tile, 2, row, pl.ds(col, 1), :] * Z

    def load_duals(source):
        for m in range(slots):
            row = source(places[m][0], places[m][1], pl.ds(places[m][2], 1))
            table[3:4, m * block : (m + 1) * block] = jnp.where(m < live, row * SCALE, DEAD)

    load_duals(lambda d, r, c: halo[d, 3, r, c, :])

    serial = lax.broadcasted_iota(jnp.int32, (ROWS, columns), 0)
    step_x = (serial // TY).astype(jnp.float32) - 0.5
    step_y = (serial % TY).astype(jnp.float32) - 0.5 * (TY - 1)
    level_z = (lax.broadcasted_iota(jnp.int32, (ROWS, Z), 1).astype(jnp.float32) + 0.5 - HALF_Z) * (1.0 / HALF_Z)

    def centres(n):
        return (2 * n + 1.0) - table[0:1, :], 0.5 * TY - table[1:2, :]

    for n in range(GROUPS):
        centre_x, centre_y = centres(n)
        base_ref[n : n + 1, :] = -SCALE * (centre_x * centre_x + centre_y * centre_y)
        plain = jnp.exp2((-2.0 * SCALE) * (step_x * centre_x + step_y * centre_y))
        plain_ref[n] = plain
        high, low = halves(plain)
        high = high.astype(jnp.float32)
        low = low.astype(jnp.bfloat16).astype(jnp.float32)
        left_ref[n, 0:16] = jnp.concatenate([high, low], axis=0).astype(jnp.bfloat16)

    def extend():
        for n in range(GROUPS):
            centre_x, centre_y = centres(n)
            plain = plain_ref[n]
            high, low = halves(plain)
            kept = high.astype(jnp.float32) + low.astype(jnp.bfloat16).astype(jnp.float32)
            deep = kept * ((table[2:3, :] - HALF_Z) * (1.0 / HALF_Z))
            first = deep.astype(jnp.bfloat16).astype(jnp.float32)
            second = (deep - first).astype(jnp.bfloat16).astype(jnp.float32)
            third = deep - first - second
            across = plain * ((centre_x + step_x) * (1.0 / UNIT_XY))
            aside = plain * ((centre_y + step_y) * (1.0 / UNIT_XY))
            flat = jnp.concatenate([across, aside], axis=0)
            high, low = halves(flat)
            left_ref[n, 16:32] = jnp.concatenate([first, second], axis=0).astype(jnp.bfloat16)
            left_ref[n, 32:48] = jnp.concatenate([third, jnp.zeros_like(third)], axis=0).astype(jnp.bfloat16)
            left_ref[n, 48:64] = high
            left_ref[n, 64:80] = low.astype(jnp.bfloat16)

    steps = lax.broadcasted_iota(jnp.int32, (CHUNK, columns), 0).astype(jnp.float32) - (0.5 * CHUNK - 0.5)

    def build(again):
        levels = [base_ref[n : n + 1, :] + table[3:4, :] for n in range(GROUPS)]
        for start in range(0, Z, CHUNK):
            at = slice(start, start + CHUNK)
            if again:
                shape = shape_ref[at, :]
            else:
                away = table[2:3, :] - (start + 0.5 * CHUNK)
                shape = steps * (away * (2.0 * SCALE)) + away * away * (-SCALE)
                shape_ref[at, :] = shape
            for n in range(GROUPS):
                score = shape + levels[n]
                g = jnp.exp2(score - (jnp.max(score, axis=1, keepdims=True) - LIFT))
                high, low = halves(g)
                g_high[n, at, :] = high
                g_low[n, at, :] = low.astype(jnp.bfloat16)

    build(False)
    pairs = []
    for n in range(GROUPS):
        found = product(left_ref[n, 0:16], g_high[n], g_low[n], NT)
        inverse = HEAD / (found[0:8] + found[8:16])
        high, low = halves(inverse)
        pairs.append(jnp.concatenate([high.astype(jnp.float32), low], axis=0).astype(jnp.bfloat16))
    total = jnp.zeros((ROWS, columns), jnp.float32)
    for n in range(GROUPS):
        found = product(pairs[n], g_high[n], g_low[n], NN)
        total = total + plain_ref[n] * (found[0:8] + found[8:16])
    rows = total_rows(total) * (1.0 / HEAD)
    shape = (side, side, block)
    inner = lax.broadcasted_iota(jnp.int32, shape, 0) * side + lax.broadcasted_iota(
        jnp.int32, shape, 1
    )
    wanted = [places[m][1] * side + places[m][2] + (side * side) * places[m][0] for m in range(slots)]
    spread = [
        jnp.broadcast_to(rows[0:1, m * block : (m + 1) * block][None], shape) for m in range(slots)
    ]
    for d in range(9):
        found = jnp.zeros(shape, jnp.float32)
        for m in range(slots):
            found = found + jnp.where(inner == wanted[m] - side * side * d, spread[m], 0.0)
        part_send[d // 3, d % 3] = found
    second = begin([wide_copy(a, b) for a, b in WIDE])
    extend()
    finish(second)
    for i in range(3):
        for j in range(3):
            mass = part_send[i, j]
            for a, b in WIDE:
                if 0 <= i - max(a, 0) < 3 - abs(a) and 0 <= j - max(b, 0) < 3 - abs(b):
                    mass = mass + part_recv[(a + 2) * 5 + b + 2, i, j]
            d = 3 * i + j
            mid_all[d] = halo[d, 3] + step_rate * (halo[d, 4] - mass)

    homeward = begin([home_copy(2, mid_all.at[4], mid_home)])
    load_duals(lambda d, r, c: mid_all[d, r, c, :])
    build(True)
    pairs = []
    for n in range(GROUPS):
        found = product(left_ref[n], g_high[n], g_low[n], NT)
        inverse = HEAD / (found[0:8] + found[8:16])
        high, low = halves(inverse)
        high = high.astype(jnp.float32)
        low = low.astype(jnp.bfloat16).astype(jnp.float32)
        deep = (high + low) * level_z
        first = deep.astype(jnp.bfloat16).astype(jnp.float32)
        second = (deep - first).astype(jnp.bfloat16).astype(jnp.float32)
        third = deep - first - second
        pairs.append(jnp.concatenate(
            [high, low, first, second, third, jnp.zeros_like(third)], axis=0
        ).astype(jnp.bfloat16))
        inverse = inverse * (1.0 / HEAD)
        offsets = (
            (found[48:56] + found[64:72]) * inverse * -UNIT_XY,
            (found[56:64] + found[72:80]) * inverse * -UNIT_XY,
            ((found[16:24] + found[24:32] + found[32:40]) * inverse - level_z) * HALF_Z,
        )
        for c in range(3):
            for r in range(2):
                disp_send[c, 2 * n + r] = offsets[c][TY * r : TY * r + TY]
        part = (slice(None), pl.ds(2 * n, 2))
        homeward += begin([home_copy(3 + n, disp_send.at[part], disp_ref.at[part])])
    sums = [jnp.zeros((ROWS, columns), jnp.float32) for _ in range(4)]
    for n in range(GROUPS):
        centre_x, centre_y = centres(n)
        found = product(pairs[n], g_high[n], g_low[n], NN)
        plain = plain_ref[n]
        mass = plain * (found[0:8] + found[8:16])
        deep = plain * (found[16:24] + found[24:32] + found[32:40])
        sums[0] = sums[0] + mass
        sums[1] = sums[1] + mass * (centre_x + step_x)
        sums[2] = sums[2] + mass * (centre_y + step_y)
        sums[3] = sums[3] + (deep * HALF_Z - mass * (table[2:3, :] - HALF_Z))
    sums = [total_rows(v) for v in sums]
    kind = serial % 4
    rows = jnp.where(
        kind < 2, jnp.where(kind == 0, sums[0], sums[1]), jnp.where(kind == 2, sums[2], sums[3])
    ) * (1.0 / HEAD)
    upper = lax.broadcasted_iota(jnp.int32, (8, block), 0) // 4
    for d in range(9):
        for v in range(side * side // 2):
            found = jnp.zeros((8, block), jnp.float32)
            for m in range(slots):
                here = upper == wanted[m] - (side * side * d + 2 * v)
                found = found + jnp.where(here, rows[:, m * block : (m + 1) * block], 0.0)
            four_send[d, 8 * v : 8 * v + 8, :] = found
    closing = begin([
        Spread(1, d, wrap(tile + d // 3 - 1), four_send.at[d], four_recv) for d in range(9)
    ])
    finish(closing)
    four = four_recv[0]
    for d in range(1, 9):
        four = four + four_recv[d]
    homeward[0].wait()
    for i in range(side * side):
        r, c = i // side, i % side
        goal = mine[4, r, c : c + 1, :]
        found = four[4 * i : 4 * i + 1]
        new_ref[r, c : c + 1, :] = mid_home[r, c : c + 1, :] + step_rate * (goal - found)
        weight = 1.0 / (found + goal)
        for k in range(3):
            shift_ref[k, r, c : c + 1, :] = four[4 * i + k + 1 : 4 * i + k + 2] * weight
    finish(homeward[1:])
    for one in opening + closing:
        one.wait_send()


def place_results(new_ref, shift_ref, disp_ref, new_out, shift_out, disp_out, sems):
    pairs = ((disp_ref, disp_out), (shift_ref, shift_out), (new_ref, new_out))
    copies = [pltpu.make_async_copy(src, dst, sems.at[n]) for n, (src, dst) in enumerate(pairs)]
    for one in copies:
        one.start()
    for one in copies:
        one.wait()


def on_device(site_frac, dual_weight, target_mass, block_list, block_count):
    side = site_frac.shape[1]
    block = site_frac.shape[3]
    columns = block_list.shape[2] * block
    f32, bf16, i32 = jnp.float32, jnp.bfloat16, jnp.int32
    vmem = pl.BlockSpec(memory_space=pltpu.VMEM)
    place = pl.BlockSpec(memory_space=pl.ANY)
    results = pl.pallas_call(
        kernel,
        out_shape=(
            pltpu.VMEM(dual_weight.shape, f32),
            pltpu.VMEM(site_frac.shape, f32),
            pltpu.VMEM((3, TX, TY, Z), f32),
        ),
        in_specs=[place] * 5,
        out_specs=(vmem, vmem, vmem),
        scratch_shapes=[
            pltpu.VMEM((5,) + dual_weight.shape, f32),
            pltpu.VMEM((9, 5) + dual_weight.shape, f32),
            pltpu.VMEM((9,) + dual_weight.shape, f32),
            pltpu.VMEM((3, 3, side, side, block), f32),
            pltpu.VMEM((25, 3, 3, side, side, block), f32),
            pltpu.VMEM((9, 4 * side * side, block), f32),
            pltpu.VMEM((9, 4 * side * side, block), f32),
            pltpu.VMEM((3, TX, TY, Z), f32),
            pltpu.VMEM(dual_weight.shape, f32),
            pltpu.SMEM(block_list.shape, i32),
            pltpu.SMEM(block_count.shape, i32),
            pltpu.SMEM(block_list.shape, i32),
            pltpu.SMEM(block_count.shape, i32),
            pltpu.VMEM((8, columns), f32),
            pltpu.VMEM((8, columns), f32),
            pltpu.VMEM((GROUPS, ROWS, columns), f32),
            pltpu.VMEM((GROUPS, 10 * ROWS, columns), bf16),
            pltpu.VMEM((Z, columns), f32),
            pltpu.VMEM((GROUPS, Z, columns), bf16),
            pltpu.VMEM((GROUPS, Z, columns), bf16),
            pltpu.SemaphoreType.DMA((25,)),
            pltpu.SemaphoreType.DMA((25,)),
            pltpu.SemaphoreType.DMA((2, 9)),
            pltpu.SemaphoreType.DMA((2, 9)),
            pltpu.SemaphoreType.DMA((3 + GROUPS,)),
            pltpu.SemaphoreType.DMA((3 + GROUPS,)),
            pltpu.SemaphoreType.DMA((5,)),
        ],
        compiler_params=pltpu.CompilerParams(collective_id=0, has_side_effects=True),
        name="transport",
    )(site_frac, dual_weight, target_mass, block_list, block_count)
    return pl.pallas_call(
        place_results,
        out_shape=tuple(jax.ShapeDtypeStruct(r.shape, f32) for r in results),
        in_specs=[vmem] * 3,
        out_specs=(pl.BlockSpec(memory_space=pltpu.HBM),) * 3,
        scratch_shapes=[pltpu.SemaphoreType.DMA((3,))],
        name="place",
    )(*[pltpu.with_memory_space_constraint(r, pltpu.VMEM) for r in results])


def solution(mesh):
    in_specs = (
        P(None, "gx", "gy", None),
        P("gx", "gy", None),
        P("gx", "gy", None),
        P("gx", "gy", None),
        P("gx", "gy"),
    )
    out_specs = (P("gx", "gy", None), P(None, "gx", "gy", None), P(None, "gx", "gy", None))
    return jax.shard_map(
        on_device, mesh=mesh, in_specs=in_specs, out_specs=out_specs, check_vma=False
    )
```

```python
import functools
import math

import jax
import jax.numpy as jnp
from jax import lax
from jax.experimental import pallas as pl
from jax.experimental.pallas import tpu as pltpu
from jax.sharding import PartitionSpec as P

TX = 4
TY = 4
Z = 256

entropy_scale = 0.5
step_rate = 0.5

SCALE = 1.0 / (entropy_scale * math.log(2.0))
DEAD = -1e30
LIFT = 40.0
HEAD = 2.0**30
UNIT_XY = 8.0
HALF_Z = 0.5 * Z
CHUNK = 32
PART = 128
WIDE = sorted([(a, b) for a in range(-2, 3) for b in range(-2, 3) if (a, b) != (0, 0)], key=lambda v: -abs(v[0]) - abs(v[1]))
GROUPS = TX // 2
ROWS = 2 * TY
NT = (((1,), (1,)), ((), ()))
NN = (((1,), (0,)), ((), ()))


def halves(value):
    high = value.astype(jnp.bfloat16)
    return high, value - high.astype(jnp.float32)


def product(left, high, low, dims):
    return lax.dot_general(
        left, high, dims, preferred_element_type=jnp.float32
    ) + lax.dot_general(left, low, dims, preferred_element_type=jnp.float32)


def total_rows(value):
    for shift in (4, 2, 1):
        value = value + pltpu.roll(value, shift, 0)
    return value


def kernel(
    frac_ref, dual_ref, target_ref, list_ref, count_ref,
    new_ref, shift_ref, disp_ref,
    mine, halo, mid_all, part_send, part_recv, four_send, four_recv, disp_send, mid_home,
    list_mine, count_mine, list_held, count_held,
    table, base_ref, plain_ref, left_ref, shape_ref, g_high, g_low,
    wide_send, wide_recv, send_sem, recv_sem, home_send, home_recv, local_sem,
):
    side = frac_ref.shape[1]
    block = frac_ref.shape[3]
    slots = list_ref.shape[2]
    columns = slots * block
    span = 3 * side
    gx, gy = lax.axis_index("gx"), lax.axis_index("gy")
    nx, ny = lax.axis_size("gx"), lax.axis_size("gy")

    half = max(nx // 2, 1)
    rest = nx - half

    def wrap(t):
        return lax.rem(t + nx, nx)

    def worker(t):
        return jnp.where(t < half, lax.rem(t + half - 1, half), half + lax.rem(t - half + nx + 1, rest))

    tile = jnp.where(gx < half, lax.rem(gx + 1, half), half + lax.rem(gx - half + rest - 1 + nx * rest, rest))

    def column(b):
        return lax.rem(gy + b + ny, ny)

    def far(a, b):
        return (worker(wrap(tile + a)), column(b))

    def wide_copy(a, b):
        here = tuple(pl.ds(max(v, 0), 3 - abs(v)) for v in (a, b))
        there = tuple(pl.ds(max(-v, 0), 3 - abs(v)) for v in (a, b))
        e = (a + 2) * 5 + b + 2
        return pltpu.make_async_remote_copy(
            src_ref=part_send.at[here], dst_ref=part_recv.at[(24 - e,) + there],
            send_sem=wide_send.at[e], recv_sem=wide_recv.at[24 - e],
            device_id=far(a, b), device_id_type=pl.DeviceIdType.MESH,
        )

    class Spread:
        def __init__(self, phase, d, where, src, dst):
            self.near = d % 3 == 1 and d != 4
            self.own = where == gx
            self.remote = pltpu.make_async_remote_copy(
                src_ref=src, dst_ref=dst.at[8 - d],
                send_sem=send_sem.at[phase, d], recv_sem=recv_sem.at[phase, 8 - d],
                device_id=(where, column(d % 3 - 1)), device_id_type=pl.DeviceIdType.MESH,
            )
            if self.near:
                self.local = pltpu.make_async_copy(src, dst.at[8 - d], recv_sem.at[phase, 8 - d])

        def start(self):
            if not self.near:
                self.remote.start()
                return
            pl.when(self.own)(self.local.start)
            pl.when(jnp.logical_not(self.own))(self.remote.start)

        def wait(self):
            self.remote.wait_recv()

        def wait_send(self):
            if not self.near:
                self.remote.wait_send()
                return
            pl.when(jnp.logical_not(self.own))(self.remote.wait_send)

    def home_copy(n, src, dst):
        return pltpu.make_async_remote_copy(
            src_ref=src, dst_ref=dst, send_sem=home_send.at[n], recv_sem=home_recv.at[n],
            device_id=(tile, gy), device_id_type=pl.DeviceIdType.MESH,
        )

    def begin(copies):
        for one in copies:
            one.start()
        return copies

    def finish(copies):
        for one in copies:
            one.wait()

    barrier = pltpu.get_barrier_semaphore()
    for a in range(-1, 2):
        for b in range(-1, 2):
            pl.semaphore_signal(
                barrier, inc=1, device_id=(wrap(tile + a), column(b)),
                device_id_type=pl.DeviceIdType.MESH,
            )
    finish(begin([
        pltpu.make_async_copy(src, dst, local_sem.at[n])
        for n, (src, dst) in enumerate([
            (frac_ref, mine.at[0:3]), (dual_ref, mine.at[3]), (target_ref, mine.at[4]),
            (list_ref, list_mine), (count_ref, count_mine),
        ])
    ]))
    pl.semaphore_wait(barrier, 9)

    listed = begin([
        pltpu.make_async_remote_copy(
            src_ref=src, dst_ref=dst, send_sem=home_send.at[n], recv_sem=home_recv.at[n],
            device_id=(worker(gx), gy), device_id_type=pl.DeviceIdType.MESH,
        )
        for n, src, dst in ((0, list_mine, list_held), (1, count_mine, count_held))
    ])
    opening = begin([
        Spread(0, d, worker(wrap(gx + d // 3 - 1)), mine, halo) for d in range(9)
    ])
    for one in listed:
        one.wait_recv()
    live = count_held[0, 0]
    places = []
    for m in range(slots):
        slot = list_held[0, 0, m]
        row, col = slot // span, slot % span
        places.append(((row // side) * 3 + col // side, row % side, col % side,
                       (row // side - 1).astype(jnp.float32) * TX,
                       (col // side - 1).astype(jnp.float32) * TY))
    finish(opening)

    for m in range(slots):
        block_tile, row, col, corner_x, corner_y = places[m]
        at = slice(m * block, (m + 1) * block)
        table[0:1, at] = halo[block_tile, 0, row, pl.ds(col, 1), :] * TX + corner_x
        table[1:2, at] = halo[block_tile, 1, row, pl.ds(col, 1), :] * TY + corner_y
        table[2:3, at] = halo[block_tile, 2, row, pl.ds(col, 1), :] * Z

    def load_duals(source):
        for m in range(slots):
            row = source(places[m][0], places[m][1], pl.ds(places[m][2], 1))
            table[3:4, m * block : (m + 1) * block] = jnp.where(m < live, row * SCALE, DEAD)

    load_duals(lambda d, r, c: halo[d, 3, r, c, :])

    serial = lax.broadcasted_iota(jnp.int32, (ROWS, columns), 0)
    step_x = (serial // TY).astype(jnp.float32) - 0.5
    step_y = (serial % TY).astype(jnp.float32) - 0.5 * (TY - 1)
    level_z = (lax.broadcasted_iota(jnp.int32, (ROWS, Z), 1).astype(jnp.float32) + 0.5 - HALF_Z) * (1.0 / HALF_Z)

    def centres(n):
        return (2 * n + 1.0) - table[0:1, :], 0.5 * TY - table[1:2, :]

    for n in range(GROUPS):
        centre_x, centre_y = centres(n)
        base_ref[n : n + 1, :] = -SCALE * (centre_x * centre_x + centre_y * centre_y)
        plain = jnp.exp2((-2.0 * SCALE) * (step_x * centre_x + step_y * centre_y))
        plain_ref[n] = plain
        high, low = halves(plain)
        high = high.astype(jnp.float32)
        low = low.astype(jnp.bfloat16).astype(jnp.float32)
        left_ref[n, 0:16] = jnp.concatenate([high, low], axis=0).astype(jnp.bfloat16)

    def extend():
        for n in range(GROUPS):
            centre_x, centre_y = centres(n)
            plain = plain_ref[n]
            high, low = halves(plain)
            kept = high.astype(jnp.float32) + low.astype(jnp.bfloat16).astype(jnp.float32)
            deep = kept * ((table[2:3, :] - HALF_Z) * (1.0 / HALF_Z))
            first = deep.astype(jnp.bfloat16).astype(jnp.float32)
            second = (deep - first).astype(jnp.bfloat16).astype(jnp.float32)
            third = deep - first - second
            across = plain * ((centre_x + step_x) * (1.0 / UNIT_XY))
            aside = plain * ((centre_y + step_y) * (1.0 / UNIT_XY))
            flat = jnp.concatenate([across, aside], axis=0)
            high, low = halves(flat)
            left_ref[n, 16:32] = jnp.concatenate([first, second], axis=0).astype(jnp.bfloat16)
            left_ref[n, 32:48] = jnp.concatenate([third, jnp.zeros_like(third)], axis=0).astype(jnp.bfloat16)
            left_ref[n, 48:64] = high
            left_ref[n, 64:80] = low.astype(jnp.bfloat16)

    steps = lax.broadcasted_iota(jnp.int32, (CHUNK, columns), 0).astype(jnp.float32) - (0.5 * CHUNK - 0.5)

    def build(again, rows):
        found = [[] for _ in range(GROUPS)]
        levels = [base_ref[n : n + 1, :] + table[3:4, :] for n in range(GROUPS)]
        for start in range(0, Z, CHUNK):
            at = slice(start, start + CHUNK)
            if again:
                shape = shape_ref[at, :]
            else:
                away = table[2:3, :] - (start + 0.5 * CHUNK)
                shape = steps * (away * (2.0 * SCALE)) + away * away * (-SCALE)
                shape_ref[at, :] = shape
            for n in range(GROUPS):
                score = shape + levels[n]
                g = jnp.exp2(score - (jnp.max(score, axis=1, keepdims=True) - LIFT))
                high, low = halves(g)
                g_high[n, at, :] = high
                g_low[n, at, :] = low.astype(jnp.bfloat16)
            if (start + CHUNK) % PART == 0:
                at = slice(start + CHUNK - PART, start + CHUNK)
                for n in range(GROUPS):
                    found[n].append(product(left_ref[n, 0:rows], g_high[n, at, :], g_low[n, at, :], NT))
        return [jnp.concatenate(parts, axis=1) for parts in found]

    sums = build(False, 16)
    pairs = []
    for n in range(GROUPS):
        found = sums[n]
        inverse = HEAD / (found[0:8] + found[8:16])
        high, low = halves(inverse)
        pairs.append(jnp.concatenate([high.astype(jnp.float32), low], axis=0).astype(jnp.bfloat16))
    total = jnp.zeros((ROWS, columns), jnp.float32)
    for n in range(GROUPS):
        found = product(pairs[n], g_high[n], g_low[n], NN)
        total = total + plain_ref[n] * (found[0:8] + found[8:16])
    rows = total_rows(total) * (1.0 / HEAD)
    shape = (side, side, block)
    inner = lax.broadcasted_iota(jnp.int32, shape, 0) * side + lax.broadcasted_iota(
        jnp.int32, shape, 1
    )
    wanted = [places[m][1] * side + places[m][2] + (side * side) * places[m][0] for m in range(slots)]
    spread = [
        jnp.broadcast_to(rows[0:1, m * block : (m + 1) * block][None], shape) for m in range(slots)
    ]
    for d in range(9):
        found = jnp.zeros(shape, jnp.float32)
        for m in range(slots):
            found = found + jnp.where(inner == wanted[m] - side * side * d, spread[m], 0.0)
        part_send[d // 3, d % 3] = found
    crossing = begin([wide_copy(a, b) for a, b in WIDE])
    extend()
    for one in crossing:
        one.wait_recv()
    for i in range(3):
        for j in range(3):
            mass = part_send[i, j]
            for a, b in WIDE:
                if 0 <= i - max(a, 0) < 3 - abs(a) and 0 <= j - max(b, 0) < 3 - abs(b):
                    mass = mass + part_recv[(a + 2) * 5 + b + 2, i, j]
            d = 3 * i + j
            mid_all[d] = halo[d, 3] + step_rate * (halo[d, 4] - mass)

    homeward = begin([home_copy(2, mid_all.at[4], mid_home)])
    load_duals(lambda d, r, c: mid_all[d, r, c, :])
    sums = build(True, 10 * ROWS)
    pairs = []
    for n in range(GROUPS):
        found = sums[n]
        inverse = HEAD / (found[0:8] + found[8:16])
        high, low = halves(inverse)
        high = high.astype(jnp.float32)
        low = low.astype(jnp.bfloat16).astype(jnp.float32)
        deep = (high + low) * level_z
        first = deep.astype(jnp.bfloat16).astype(jnp.float32)
        second = (deep - first).astype(jnp.bfloat16).astype(jnp.float32)
        third = deep - first - second
        pairs.append(jnp.concatenate(
            [high, low, first, second, third, jnp.zeros_like(third)], axis=0
        ).astype(jnp.bfloat16))
        inverse = inverse * (1.0 / HEAD)
        offsets = (
            (found[48:56] + found[64:72]) * inverse * -UNIT_XY,
            (found[56:64] + found[72:80]) * inverse * -UNIT_XY,
            ((found[16:24] + found[24:32] + found[32:40]) * inverse - level_z) * HALF_Z,
        )
        for c in range(3):
            for r in range(2):
                disp_send[c, 2 * n + r] = offsets[c][TY * r : TY * r + TY]
        part = (slice(None), pl.ds(2 * n, 2))
        homeward += begin([home_copy(3 + n, disp_send.at[part], disp_ref.at[part])])
    sums = [jnp.zeros((ROWS, columns), jnp.float32) for _ in range(4)]
    for n in range(GROUPS):
        centre_x, centre_y = centres(n)
        found = product(pairs[n], g_high[n], g_low[n], NN)
        plain = plain_ref[n]
        mass = plain * (found[0:8] + found[8:16])
        deep = plain * (found[16:24] + found[24:32] + found[32:40])
        sums[0] = sums[0] + mass
        sums[1] = sums[1] + mass * (centre_x + step_x)
        sums[2] = sums[2] + mass * (centre_y + step_y)
        sums[3] = sums[3] + (deep * HALF_Z - mass * (table[2:3, :] - HALF_Z))
    sums = [total_rows(v) for v in sums]
    kind = serial % 4
    rows = jnp.where(
        kind < 2, jnp.where(kind == 0, sums[0], sums[1]), jnp.where(kind == 2, sums[2], sums[3])
    ) * (1.0 / HEAD)
    upper = lax.broadcasted_iota(jnp.int32, (8, block), 0) // 4
    for d in range(9):
        for v in range(side * side // 2):
            found = jnp.zeros((8, block), jnp.float32)
            for m in range(slots):
                here = upper == wanted[m] - (side * side * d + 2 * v)
                found = found + jnp.where(here, rows[:, m * block : (m + 1) * block], 0.0)
            four_send[d, 8 * v : 8 * v + 8, :] = found
    closing = begin([
        Spread(1, d, wrap(tile + d // 3 - 1), four_send.at[d], four_recv) for d in range(9)
    ])
    for one in listed + opening + crossing:
        one.wait_send()
    finish(closing)
    four = four_recv[0]
    for d in range(1, 9):
        four = four + four_recv[d]
    homeward[0].wait()
    for i in range(side * side):
        r, c = i // side, i % side
        goal = mine[4, r, c : c + 1, :]
        found = four[4 * i : 4 * i + 1]
        new_ref[r, c : c + 1, :] = mid_home[r, c : c + 1, :] + step_rate * (goal - found)
        weight = 1.0 / (found + goal)
        for k in range(3):
            shift_ref[k, r, c : c + 1, :] = four[4 * i + k + 1 : 4 * i + k + 2] * weight
    finish(homeward[1:])
    for one in closing:
        one.wait_send()


def place_results(new_ref, shift_ref, disp_ref, new_out, shift_out, disp_out, sems):
    pairs = ((disp_ref, disp_out), (shift_ref, shift_out), (new_ref, new_out))
    copies = [pltpu.make_async_copy(src, dst, sems.at[n]) for n, (src, dst) in enumerate(pairs)]
    for one in copies:
        one.start()
    for one in copies:
        one.wait()


def on_device(site_frac, dual_weight, target_mass, block_list, block_count):
    side = site_frac.shape[1]
    block = site_frac.shape[3]
    columns = block_list.shape[2] * block
    f32, bf16, i32 = jnp.float32, jnp.bfloat16, jnp.int32
    vmem = pl.BlockSpec(memory_space=pltpu.VMEM)
    place = pl.BlockSpec(memory_space=pl.ANY)
    results = pl.pallas_call(
        kernel,
        out_shape=(
            pltpu.VMEM(dual_weight.shape, f32),
            pltpu.VMEM(site_frac.shape, f32),
            pltpu.VMEM((3, TX, TY, Z), f32),
        ),
        in_specs=[place] * 5,
        out_specs=(vmem, vmem, vmem),
        scratch_shapes=[
            pltpu.VMEM((5,) + dual_weight.shape, f32),
            pltpu.VMEM((9, 5) + dual_weight.shape, f32),
            pltpu.VMEM((9,) + dual_weight.shape, f32),
            pltpu.VMEM((3, 3, side, side, block), f32),
            pltpu.VMEM((25, 3, 3, side, side, block), f32),
            pltpu.VMEM((9, 4 * side * side, block), f32),
            pltpu.VMEM((9, 4 * side * side, block), f32),
            pltpu.VMEM((3, TX, TY, Z), f32),
            pltpu.VMEM(dual_weight.shape, f32),
            pltpu.SMEM(block_list.shape, i32),
            pltpu.SMEM(block_count.shape, i32),
            pltpu.SMEM(block_list.shape, i32),
            pltpu.SMEM(block_count.shape, i32),
            pltpu.VMEM((8, columns), f32),
            pltpu.VMEM((8, columns), f32),
            pltpu.VMEM((GROUPS, ROWS, columns), f32),
            pltpu.VMEM((GROUPS, 10 * ROWS, columns), bf16),
            pltpu.VMEM((Z, columns), f32),
            pltpu.VMEM((GROUPS, Z, columns), bf16),
            pltpu.VMEM((GROUPS, Z, columns), bf16),
            pltpu.SemaphoreType.DMA((25,)),
            pltpu.SemaphoreType.DMA((25,)),
            pltpu.SemaphoreType.DMA((2, 9)),
            pltpu.SemaphoreType.DMA((2, 9)),
            pltpu.SemaphoreType.DMA((3 + GROUPS,)),
            pltpu.SemaphoreType.DMA((3 + GROUPS,)),
            pltpu.SemaphoreType.DMA((5,)),
        ],
        compiler_params=pltpu.CompilerParams(collective_id=0, has_side_effects=True),
        name="transport",
    )(site_frac, dual_weight, target_mass, block_list, block_count)
    return pl.pallas_call(
        place_results,
        out_shape=tuple(jax.ShapeDtypeStruct(r.shape, f32) for r in results),
        in_specs=[vmem] * 3,
        out_specs=(pl.BlockSpec(memory_space=pltpu.HBM),) * 3,
        scratch_shapes=[pltpu.SemaphoreType.DMA((3,))],
        name="place",
    )(*[pltpu.with_memory_space_constraint(r, pltpu.VMEM) for r in results])


def solution(mesh):
    in_specs = (
        P(None, "gx", "gy", None),
        P("gx", "gy", None),
        P("gx", "gy", None),
        P("gx", "gy", None),
        P("gx", "gy"),
    )
    out_specs = (P("gx", "gy", None), P(None, "gx", "gy", None), P(None, "gx", "gy", None))
    return jax.shard_map(
        on_device, mesh=mesh, in_specs=in_specs, out_specs=out_specs, check_vma=False
    )
```

```python
import functools
import math

import jax
import jax.numpy as jnp
from jax import lax
from jax.experimental import pallas as pl
from jax.experimental.pallas import tpu as pltpu
from jax.sharding import PartitionSpec as P

TX = 4
TY = 4
Z = 256

entropy_scale = 0.5
step_rate = 0.5

SCALE = 1.0 / (entropy_scale * math.log(2.0))
DEAD = -1e30
LIFT = 40.0
HEAD = 2.0**30
UNIT_XY = 8.0
HALF_Z = 0.5 * Z
CHUNK = 32
PART = 128
WIDE = sorted([(a, b) for a in range(-2, 3) for b in range(-2, 3) if (a, b) != (0, 0)], key=lambda v: -abs(v[0]) - abs(v[1]))
GROUPS = TX // 2
ROWS = 2 * TY
NT = (((1,), (1,)), ((), ()))
NN = (((1,), (0,)), ((), ()))


def halves(value):
    high = value.astype(jnp.bfloat16)
    return high, value - high.astype(jnp.float32)


def product(left, high, low, dims):
    return lax.dot_general(
        left, high, dims, preferred_element_type=jnp.float32
    ) + lax.dot_general(left, low, dims, preferred_element_type=jnp.float32)


def total_rows(value):
    for shift in (4, 2, 1):
        value = value + pltpu.roll(value, shift, 0)
    return value


def kernel(
    frac_ref, dual_ref, target_ref, list_ref, count_ref,
    new_ref, shift_ref, disp_ref,
    mine, halo, mid_all, part_send, part_recv, four_send, four_recv, disp_send, mid_home,
    list_mine, count_mine, list_held, count_held,
    table, base_ref, plain_ref, left_ref, shape_ref, g_high, g_low,
    wide_send, wide_recv, send_sem, recv_sem, home_send, home_recv, local_sem,
):
    side = frac_ref.shape[1]
    block = frac_ref.shape[3]
    slots = list_ref.shape[2]
    columns = slots * block
    span = 3 * side
    gx, gy = lax.axis_index("gx"), lax.axis_index("gy")
    nx, ny = lax.axis_size("gx"), lax.axis_size("gy")

    half = max(nx // 2, 1)
    rest = nx - half

    def wrap(t):
        return lax.rem(t + nx, nx)

    def worker(t):
        return jnp.where(t < half, lax.rem(t + half - 1, half), half + lax.rem(t - half + nx + 1, rest))

    tile = jnp.where(gx < half, lax.rem(gx + 1, half), half + lax.rem(gx - half + rest - 1 + nx * rest, rest))

    def column(b):
        return lax.rem(gy + b + ny, ny)

    def far(a, b):
        return (worker(wrap(tile + a)), column(b))

    def wide_copy(a, b):
        here = tuple(pl.ds(max(v, 0), 3 - abs(v)) for v in (a, b))
        there = tuple(pl.ds(max(-v, 0), 3 - abs(v)) for v in (a, b))
        e = (a + 2) * 5 + b + 2
        return pltpu.make_async_remote_copy(
            src_ref=part_send.at[here], dst_ref=part_recv.at[(24 - e,) + there],
            send_sem=wide_send.at[e], recv_sem=wide_recv.at[24 - e],
            device_id=far(a, b), device_id_type=pl.DeviceIdType.MESH,
        )

    class Spread:
        def __init__(self, phase, d, where, src, dst):
            self.near = d % 3 == 1 and d != 4
            self.own = where == gx
            self.remote = pltpu.make_async_remote_copy(
                src_ref=src, dst_ref=dst.at[8 - d],
                send_sem=send_sem.at[phase, d], recv_sem=recv_sem.at[phase, 8 - d],
                device_id=(where, column(d % 3 - 1)), device_id_type=pl.DeviceIdType.MESH,
            )
            if self.near:
                self.local = pltpu.make_async_copy(src, dst.at[8 - d], recv_sem.at[phase, 8 - d])

        def start(self):
            if not self.near:
                self.remote.start()
                return
            pl.when(self.own)(self.local.start)
            pl.when(jnp.logical_not(self.own))(self.remote.start)

        def wait(self):
            self.remote.wait_recv()

        def wait_send(self):
            if not self.near:
                self.remote.wait_send()
                return
            pl.when(jnp.logical_not(self.own))(self.remote.wait_send)

    def home_copy(n, src, dst):
        return pltpu.make_async_remote_copy(
            src_ref=src, dst_ref=dst, send_sem=home_send.at[n], recv_sem=home_recv.at[n],
            device_id=(tile, gy), device_id_type=pl.DeviceIdType.MESH,
        )

    def begin(copies):
        for one in copies:
            one.start()
        return copies

    def finish(copies):
        for one in copies:
            one.wait()

    barrier = pltpu.get_barrier_semaphore()
    for a in range(-1, 2):
        for b in range(-1, 2):
            pl.semaphore_signal(
                barrier, inc=1, device_id=(wrap(tile + a), column(b)),
                device_id_type=pl.DeviceIdType.MESH,
            )
    finish(begin([
        pltpu.make_async_copy(src, dst, local_sem.at[n])
        for n, (src, dst) in enumerate([
            (frac_ref, mine.at[0:3]), (dual_ref, mine.at[3]), (target_ref, mine.at[4]),
            (list_ref, list_mine), (count_ref, count_mine),
        ])
    ]))
    pl.semaphore_wait(barrier, 9)

    listed = begin([
        pltpu.make_async_remote_copy(
            src_ref=src, dst_ref=dst, send_sem=home_send.at[n], recv_sem=home_recv.at[n],
            device_id=(worker(gx), gy), device_id_type=pl.DeviceIdType.MESH,
        )
        for n, src, dst in ((0, list_mine, list_held), (1, count_mine, count_held))
    ])
    opening = begin([
        Spread(0, d, worker(wrap(gx + d // 3 - 1)), mine, halo) for d in (0, 2, 6, 8, 1, 7, 3, 5, 4)
    ])
    for one in listed:
        one.wait_recv()
    live = count_held[0, 0]
    places = []
    for m in range(slots):
        slot = list_held[0, 0, m]
        row, col = slot // span, slot % span
        places.append(((row // side) * 3 + col // side, row % side, col % side,
                       (row // side - 1).astype(jnp.float32) * TX,
                       (col // side - 1).astype(jnp.float32) * TY))
    finish(opening)

    for m in range(slots):
        block_tile, row, col, corner_x, corner_y = places[m]
        at = slice(m * block, (m + 1) * block)
        table[0:1, at] = halo[block_tile, 0, row, pl.ds(col, 1), :] * TX + corner_x
        table[1:2, at] = halo[block_tile, 1, row, pl.ds(col, 1), :] * TY + corner_y
        table[2:3, at] = halo[block_tile, 2, row, pl.ds(col, 1), :] * Z

    def load_duals(source):
        for m in range(slots):
            row = source(places[m][0], places[m][1], pl.ds(places[m][2], 1))
            table[3:4, m * block : (m + 1) * block] = jnp.where(m < live, row * SCALE, DEAD)

    load_duals(lambda d, r, c: halo[d, 3, r, c, :])

    serial = lax.broadcasted_iota(jnp.int32, (ROWS, columns), 0)
    step_x = (serial // TY).astype(jnp.float32) - 0.5
    step_y = (serial % TY).astype(jnp.float32) - 0.5 * (TY - 1)
    level_z = (lax.broadcasted_iota(jnp.int32, (ROWS, Z), 1).astype(jnp.float32) + 0.5 - HALF_Z) * (1.0 / HALF_Z)

    def centres(n):
        return (2 * n + 1.0) - table[0:1, :], 0.5 * TY - table[1:2, :]

    for n in range(GROUPS):
        centre_x, centre_y = centres(n)
        base_ref[n : n + 1, :] = -SCALE * (centre_x * centre_x + centre_y * centre_y)
        plain = jnp.exp2((-2.0 * SCALE) * (step_x * centre_x + step_y * centre_y))
        plain_ref[n] = plain
        high, low = halves(plain)
        high = high.astype(jnp.float32)
        low = low.astype(jnp.bfloat16).astype(jnp.float32)
        left_ref[n, 0:16] = jnp.concatenate([high, low], axis=0).astype(jnp.bfloat16)

    def extend():
        for n in range(GROUPS):
            centre_x, centre_y = centres(n)
            plain = plain_ref[n]
            high, low = halves(plain)
            kept = high.astype(jnp.float32) + low.astype(jnp.bfloat16).astype(jnp.float32)
            deep = kept * ((table[2:3, :] - HALF_Z) * (1.0 / HALF_Z))
            first = deep.astype(jnp.bfloat16).astype(jnp.float32)
            second = (deep - first).astype(jnp.bfloat16).astype(jnp.float32)
            third = deep - first - second
            across = plain * ((centre_x + step_x) * (1.0 / UNIT_XY))
            aside = plain * ((centre_y + step_y) * (1.0 / UNIT_XY))
            flat = jnp.concatenate([across, aside], axis=0)
            high, low = halves(flat)
            left_ref[n, 16:32] = jnp.concatenate([first, second], axis=0).astype(jnp.bfloat16)
            left_ref[n, 32:48] = jnp.concatenate([third, jnp.zeros_like(third)], axis=0).astype(jnp.bfloat16)
            left_ref[n, 48:64] = high
            left_ref[n, 64:80] = low.astype(jnp.bfloat16)

    steps = lax.broadcasted_iota(jnp.int32, (CHUNK, columns), 0).astype(jnp.float32) - (0.5 * CHUNK - 0.5)

    def build(again, rows):
        found = [[] for _ in range(GROUPS)]
        levels = [base_ref[n : n + 1, :] + table[3:4, :] for n in range(GROUPS)]
        for start in range(0, Z, CHUNK):
            at = slice(start, start + CHUNK)
            if again:
                shape = shape_ref[at, :]
            else:
                away = table[2:3, :] - (start + 0.5 * CHUNK)
                shape = steps * (away * (2.0 * SCALE)) + away * away * (-SCALE)
                shape_ref[at, :] = shape
            for n in range(GROUPS):
                score = shape + levels[n]
                g = jnp.exp2(score - (jnp.max(score, axis=1, keepdims=True) - LIFT))
                high, low = halves(g)
                g_high[n, at, :] = high
                g_low[n, at, :] = low.astype(jnp.bfloat16)
            if (start + CHUNK) % PART == 0:
                at = slice(start + CHUNK - PART, start + CHUNK)
                for n in range(GROUPS):
                    found[n].append(product(left_ref[n, 0:rows], g_high[n, at, :], g_low[n, at, :], NT))
        return [jnp.concatenate(parts, axis=1) for parts in found]

    sums = build(False, 16)
    pairs = []
    for n in range(GROUPS):
        found = sums[n]
        inverse = HEAD / (found[0:8] + found[8:16])
        high, low = halves(inverse)
        pairs.append(jnp.concatenate([high.astype(jnp.float32), low], axis=0).astype(jnp.bfloat16))
    total = jnp.zeros((ROWS, columns), jnp.float32)
    for n in range(GROUPS):
        found = product(pairs[n], g_high[n], g_low[n], NN)
        total = total + plain_ref[n] * (found[0:8] + found[8:16])
    rows = total_rows(total) * (1.0 / HEAD)
    shape = (side, side, block)
    inner = lax.broadcasted_iota(jnp.int32, shape, 0) * side + lax.broadcasted_iota(
        jnp.int32, shape, 1
    )
    wanted = [places[m][1] * side + places[m][2] + (side * side) * places[m][0] for m in range(slots)]
    spread = [
        jnp.broadcast_to(rows[0:1, m * block : (m + 1) * block][None], shape) for m in range(slots)
    ]
    for d in range(9):
        found = jnp.zeros(shape, jnp.float32)
        for m in range(slots):
            found = found + jnp.where(inner == wanted[m] - side * side * d, spread[m], 0.0)
        part_send[d // 3, d % 3] = found
    crossing = begin([wide_copy(a, b) for a, b in WIDE])
    extend()
    for one in crossing:
        one.wait_recv()
    for i in range(3):
        for j in range(3):
            mass = part_send[i, j]
            for a, b in WIDE:
                if 0 <= i - max(a, 0) < 3 - abs(a) and 0 <= j - max(b, 0) < 3 - abs(b):
                    mass = mass + part_recv[(a + 2) * 5 + b + 2, i, j]
            d = 3 * i + j
            mid_all[d] = halo[d, 3] + step_rate * (halo[d, 4] - mass)

    homeward = begin([home_copy(2, mid_all.at[4], mid_home)])
    load_duals(lambda d, r, c: mid_all[d, r, c, :])
    sums = build(True, 10 * ROWS)
    pairs = []
    for n in range(GROUPS):
        found = sums[n]
        inverse = HEAD / (found[0:8] + found[8:16])
        high, low = halves(inverse)
        high = high.astype(jnp.float32)
        low = low.astype(jnp.bfloat16).astype(jnp.float32)
        deep = (high + low) * level_z
        first = deep.astype(jnp.bfloat16).astype(jnp.float32)
        second = (deep - first).astype(jnp.bfloat16).astype(jnp.float32)
        third = deep - first - second
        pairs.append(jnp.concatenate(
            [high, low, first, second, third, jnp.zeros_like(third)], axis=0
        ).astype(jnp.bfloat16))
        inverse = inverse * (1.0 / HEAD)
        offsets = (
            (found[48:56] + found[64:72]) * inverse * -UNIT_XY,
            (found[56:64] + found[72:80]) * inverse * -UNIT_XY,
            ((found[16:24] + found[24:32] + found[32:40]) * inverse - level_z) * HALF_Z,
        )
        for c in range(3):
            for r in range(2):
                disp_send[c, 2 * n + r] = offsets[c][TY * r : TY * r + TY]
        part = (slice(None), pl.ds(2 * n, 2))
        homeward += begin([home_copy(3 + n, disp_send.at[part], disp_ref.at[part])])
    sums = [jnp.zeros((ROWS, columns), jnp.float32) for _ in range(4)]
    for n in range(GROUPS):
        centre_x, centre_y = centres(n)
        found = product(pairs[n], g_high[n], g_low[n], NN)
        plain = plain_ref[n]
        mass = plain * (found[0:8] + found[8:16])
        deep = plain * (found[16:24] + found[24:32] + found[32:40])
        sums[0] = sums[0] + mass
        sums[1] = sums[1] + mass * (centre_x + step_x)
        sums[2] = sums[2] + mass * (centre_y + step_y)
        sums[3] = sums[3] + (deep * HALF_Z - mass * (table[2:3, :] - HALF_Z))
    sums = [total_rows(v) for v in sums]
    kind = serial % 4
    rows = jnp.where(
        kind < 2, jnp.where(kind == 0, sums[0], sums[1]), jnp.where(kind == 2, sums[2], sums[3])
    ) * (1.0 / HEAD)
    upper = lax.broadcasted_iota(jnp.int32, (8, block), 0) // 4
    for d in range(9):
        for v in range(side * side // 2):
            found = jnp.zeros((8, block), jnp.float32)
            for m in range(slots):
                here = upper == wanted[m] - (side * side * d + 2 * v)
                found = found + jnp.where(here, rows[:, m * block : (m + 1) * block], 0.0)
            four_send[d, 8 * v : 8 * v + 8, :] = found
    closing = begin([
        Spread(1, d, wrap(tile + d // 3 - 1), four_send.at[d], four_recv) for d in range(9)
    ])
    for one in listed + opening + crossing:
        one.wait_send()
    finish(closing)
    four = four_recv[0]
    for d in range(1, 9):
        four = four + four_recv[d]
    homeward[0].wait()
    for i in range(side * side):
        r, c = i // side, i % side
        goal = mine[4, r, c : c + 1, :]
        found = four[4 * i : 4 * i + 1]
        new_ref[r, c : c + 1, :] = mid_home[r, c : c + 1, :] + step_rate * (goal - found)
        weight = 1.0 / (found + goal)
        for k in range(3):
            shift_ref[k, r, c : c + 1, :] = four[4 * i + k + 1 : 4 * i + k + 2] * weight
    finish(homeward[1:])
    for one in closing:
        one.wait_send()


def place_results(new_ref, shift_ref, disp_ref, new_out, shift_out, disp_out, sems):
    pairs = ((disp_ref, disp_out), (shift_ref, shift_out), (new_ref, new_out))
    copies = [pltpu.make_async_copy(src, dst, sems.at[n]) for n, (src, dst) in enumerate(pairs)]
    for one in copies:
        one.start()
    for one in copies:
        one.wait()


def on_device(site_frac, dual_weight, target_mass, block_list, block_count):
    side = site_frac.shape[1]
    block = site_frac.shape[3]
    columns = block_list.shape[2] * block
    f32, bf16, i32 = jnp.float32, jnp.bfloat16, jnp.int32
    vmem = pl.BlockSpec(memory_space=pltpu.VMEM)
    place = pl.BlockSpec(memory_space=pl.ANY)
    results = pl.pallas_call(
        kernel,
        out_shape=(
            pltpu.VMEM(dual_weight.shape, f32),
            pltpu.VMEM(site_frac.shape, f32),
            pltpu.VMEM((3, TX, TY, Z), f32),
        ),
        in_specs=[place] * 5,
        out_specs=(vmem, vmem, vmem),
        scratch_shapes=[
            pltpu.VMEM((5,) + dual_weight.shape, f32),
            pltpu.VMEM((9, 5) + dual_weight.shape, f32),
            pltpu.VMEM((9,) + dual_weight.shape, f32),
            pltpu.VMEM((3, 3, side, side, block), f32),
            pltpu.VMEM((25, 3, 3, side, side, block), f32),
            pltpu.VMEM((9, 4 * side * side, block), f32),
            pltpu.VMEM((9, 4 * side * side, block), f32),
            pltpu.VMEM((3, TX, TY, Z), f32),
            pltpu.VMEM(dual_weight.shape, f32),
            pltpu.SMEM(block_list.shape, i32),
            pltpu.SMEM(block_count.shape, i32),
            pltpu.SMEM(block_list.shape, i32),
            pltpu.SMEM(block_count.shape, i32),
            pltpu.VMEM((8, columns), f32),
            pltpu.VMEM((8, columns), f32),
            pltpu.VMEM((GROUPS, ROWS, columns), f32),
            pltpu.VMEM((GROUPS, 10 * ROWS, columns), bf16),
            pltpu.VMEM((Z, columns), f32),
            pltpu.VMEM((GROUPS, Z, columns), bf16),
            pltpu.VMEM((GROUPS, Z, columns), bf16),
            pltpu.SemaphoreType.DMA((25,)),
            pltpu.SemaphoreType.DMA((25,)),
            pltpu.SemaphoreType.DMA((2, 9)),
            pltpu.SemaphoreType.DMA((2, 9)),
            pltpu.SemaphoreType.DMA((3 + GROUPS,)),
            pltpu.SemaphoreType.DMA((3 + GROUPS,)),
            pltpu.SemaphoreType.DMA((5,)),
        ],
        compiler_params=pltpu.CompilerParams(collective_id=0, has_side_effects=True),
        name="transport",
    )(site_frac, dual_weight, target_mass, block_list, block_count)
    return pl.pallas_call(
        place_results,
        out_shape=tuple(jax.ShapeDtypeStruct(r.shape, f32) for r in results),
        in_specs=[vmem] * 3,
        out_specs=(pl.BlockSpec(memory_space=pltpu.HBM),) * 3,
        scratch_shapes=[pltpu.SemaphoreType.DMA((3,))],
        name="place",
    )(*[pltpu.with_memory_space_constraint(r, pltpu.VMEM) for r in results])


def solution(mesh):
    in_specs = (
        P(None, "gx", "gy", None),
        P("gx", "gy", None),
        P("gx", "gy", None),
        P("gx", "gy", None),
        P("gx", "gy"),
    )
    out_specs = (P("gx", "gy", None), P(None, "gx", "gy", None), P(None, "gx", "gy", None))
    return jax.shard_map(
        on_device, mesh=mesh, in_specs=in_specs, out_specs=out_specs, check_vma=False
    )
```

```python
import functools
import math

import jax
import jax.numpy as jnp
from jax import lax
from jax.experimental import pallas as pl
from jax.experimental.pallas import tpu as pltpu
from jax.sharding import PartitionSpec as P

TX = 4
TY = 4
Z = 256

entropy_scale = 0.5
step_rate = 0.5

SCALE = 1.0 / (entropy_scale * math.log(2.0))
DEAD = -1e30
LIFT = 40.0
HEAD = 2.0**30
UNIT_XY = 8.0
HALF_Z = 0.5 * Z
CHUNK = 32
PART = 128
WIDE = sorted([(a, b) for a in range(-2, 3) for b in range(-2, 3) if (a, b) != (0, 0)], key=lambda v: -abs(v[0]) - abs(v[1]))
GROUPS = TX // 2
ROWS = 2 * TY
NT = (((1,), (1,)), ((), ()))
NN = (((1,), (0,)), ((), ()))


def halves(value):
    high = value.astype(jnp.bfloat16)
    return high, value - high.astype(jnp.float32)


def product(left, high, low, dims):
    return lax.dot_general(
        left, high, dims, preferred_element_type=jnp.float32
    ) + lax.dot_general(left, low, dims, preferred_element_type=jnp.float32)


def total_rows(value):
    for shift in (4, 2, 1):
        value = value + pltpu.roll(value, shift, 0)
    return value


def kernel(
    frac_ref, dual_ref, target_ref, list_ref, count_ref,
    new_ref, shift_ref, disp_ref,
    mine, halo, mid_all, part_send, part_recv, four_send, four_recv, disp_send, mid_home,
    list_mine, count_mine, list_held, count_held,
    table, base_ref, plain_ref, left_ref, shape_ref, g_high, g_low,
    wide_send, wide_recv, send_sem, recv_sem, home_send, home_recv, local_sem,
):
    side = frac_ref.shape[1]
    block = frac_ref.shape[3]
    slots = list_ref.shape[2]
    columns = slots * block
    span = 3 * side
    gx, gy = lax.axis_index("gx"), lax.axis_index("gy")
    nx, ny = lax.axis_size("gx"), lax.axis_size("gy")

    half = max(nx // 2, 1)
    rest = nx - half

    def wrap(t):
        return lax.rem(t + nx, nx)

    def worker(t):
        return jnp.where(t < half, lax.rem(t + half - 1, half), half + lax.rem(t - half + nx + 1, rest))

    tile = jnp.where(gx < half, lax.rem(gx + 1, half), half + lax.rem(gx - half + rest - 1 + nx * rest, rest))

    def column(b):
        return lax.rem(gy + b + ny, ny)

    def far(a, b):
        return (worker(wrap(tile + a)), column(b))

    def wide_copy(a, b):
        here = tuple(pl.ds(max(v, 0), 3 - abs(v)) for v in (a, b))
        there = tuple(pl.ds(max(-v, 0), 3 - abs(v)) for v in (a, b))
        e = (a + 2) * 5 + b + 2
        return pltpu.make_async_remote_copy(
            src_ref=part_send.at[here], dst_ref=part_recv.at[(24 - e,) + there],
            send_sem=wide_send.at[e], recv_sem=wide_recv.at[24 - e],
            device_id=far(a, b), device_id_type=pl.DeviceIdType.MESH,
        )

    class Spread:
        def __init__(self, phase, d, where, src, dst):
            self.near = d % 3 == 1 and d != 4
            self.own = where == gx
            self.remote = pltpu.make_async_remote_copy(
                src_ref=src, dst_ref=dst.at[8 - d],
                send_sem=send_sem.at[phase, d], recv_sem=recv_sem.at[phase, 8 - d],
                device_id=(where, column(d % 3 - 1)), device_id_type=pl.DeviceIdType.MESH,
            )
            if self.near:
                self.local = pltpu.make_async_copy(src, dst.at[8 - d], recv_sem.at[phase, 8 - d])

        def start(self):
            if not self.near:
                self.remote.start()
                return
            pl.when(self.own)(self.local.start)
            pl.when(jnp.logical_not(self.own))(self.remote.start)

        def wait(self):
            self.remote.wait_recv()

        def wait_send(self):
            if not self.near:
                self.remote.wait_send()
                return
            pl.when(jnp.logical_not(self.own))(self.remote.wait_send)

    def home_copy(n, src, dst):
        return pltpu.make_async_remote_copy(
            src_ref=src, dst_ref=dst, send_sem=home_send.at[n], recv_sem=home_recv.at[n],
            device_id=(tile, gy), device_id_type=pl.DeviceIdType.MESH,
        )

    def begin(copies):
        for one in copies:
            one.start()
        return copies

    def finish(copies):
        for one in copies:
            one.wait()

    barrier = pltpu.get_barrier_semaphore()
    for a in range(-1, 2):
        for b in range(-1, 2):
            pl.semaphore_signal(
                barrier, inc=1, device_id=(wrap(tile + a), column(b)),
                device_id_type=pl.DeviceIdType.MESH,
            )
    finish(begin([
        pltpu.make_async_copy(src, dst, local_sem.at[n])
        for n, (src, dst) in enumerate([
            (frac_ref, mine.at[0:3]), (dual_ref, mine.at[3]), (target_ref, mine.at[4]),
            (list_ref, list_mine), (count_ref, count_mine),
        ])
    ]))
    pl.semaphore_wait(barrier, 9)

    listed = begin([
        pltpu.make_async_remote_copy(
            src_ref=src, dst_ref=dst, send_sem=home_send.at[n], recv_sem=home_recv.at[n],
            device_id=(worker(gx), gy), device_id_type=pl.DeviceIdType.MESH,
        )
        for n, src, dst in ((0, list_mine, list_held), (1, count_mine, count_held))
    ])
    opening = begin([
        Spread(0, d, worker(wrap(gx + d // 3 - 1)), mine, halo) for d in (0, 2, 6, 8, 1, 7, 3, 5, 4)
    ])
    for one in listed:
        one.wait_recv()
    live = count_held[0, 0]
    places = []
    for m in range(slots):
        slot = list_held[0, 0, m]
        row, col = slot // span, slot % span
        places.append(((row // side) * 3 + col // side, row % side, col % side,
                       (row // side - 1).astype(jnp.float32) * TX,
                       (col // side - 1).astype(jnp.float32) * TY))
    finish(opening)

    for m in range(slots):
        block_tile, row, col, corner_x, corner_y = places[m]
        at = slice(m * block, (m + 1) * block)
        table[0:1, at] = halo[block_tile, 0, row, pl.ds(col, 1), :] * TX + corner_x
        table[1:2, at] = halo[block_tile, 1, row, pl.ds(col, 1), :] * TY + corner_y
        table[2:3, at] = halo[block_tile, 2, row, pl.ds(col, 1), :] * Z

    def load_duals(source):
        for m in range(slots):
            row = source(places[m][0], places[m][1], pl.ds(places[m][2], 1))
            table[3:4, m * block : (m + 1) * block] = jnp.where(m < live, row * SCALE, DEAD)

    load_duals(lambda d, r, c: halo[d, 3, r, c, :])

    serial = lax.broadcasted_iota(jnp.int32, (ROWS, columns), 0)
    step_x = (serial // TY).astype(jnp.float32) - 0.5
    step_y = (serial % TY).astype(jnp.float32) - 0.5 * (TY - 1)
    level_z = (lax.broadcasted_iota(jnp.int32, (ROWS, Z), 1).astype(jnp.float32) + 0.5 - HALF_Z) * (1.0 / HALF_Z)

    def centres(n):
        return (2 * n + 1.0) - table[0:1, :], 0.5 * TY - table[1:2, :]

    for n in range(GROUPS):
        centre_x, centre_y = centres(n)
        base_ref[n : n + 1, :] = -SCALE * (centre_x * centre_x + centre_y * centre_y)
        plain = jnp.exp2((-2.0 * SCALE) * (step_x * centre_x + step_y * centre_y))
        plain_ref[n] = plain
        high, low = halves(plain)
        high = high.astype(jnp.float32)
        low = low.astype(jnp.bfloat16).astype(jnp.float32)
        left_ref[n, 0:16] = jnp.concatenate([high, low], axis=0).astype(jnp.bfloat16)

    def extend():
        for n in range(GROUPS):
            centre_x, centre_y = centres(n)
            plain = plain_ref[n]
            high, low = halves(plain)
            kept = high.astype(jnp.float32) + low.astype(jnp.bfloat16).astype(jnp.float32)
            deep = kept * ((table[2:3, :] - HALF_Z) * (1.0 / HALF_Z))
            first = deep.astype(jnp.bfloat16).astype(jnp.float32)
            second = (deep - first).astype(jnp.bfloat16).astype(jnp.float32)
            third = deep - first - second
            across = plain * ((centre_x + step_x) * (1.0 / UNIT_XY))
            aside = plain * ((centre_y + step_y) * (1.0 / UNIT_XY))
            flat = jnp.concatenate([across, aside], axis=0)
            high, low = halves(flat)
            left_ref[n, 16:32] = jnp.concatenate([first, second], axis=0).astype(jnp.bfloat16)
            left_ref[n, 32:48] = jnp.concatenate([third, jnp.zeros_like(third)], axis=0).astype(jnp.bfloat16)
            left_ref[n, 48:64] = high
            left_ref[n, 64:80] = low.astype(jnp.bfloat16)

    steps = lax.broadcasted_iota(jnp.int32, (CHUNK, columns), 0).astype(jnp.float32) - (0.5 * CHUNK - 0.5)

    def build(again, rows):
        found = [[] for _ in range(GROUPS)]
        levels = [base_ref[n : n + 1, :] + table[3:4, :] for n in range(GROUPS)]
        for start in range(0, Z, CHUNK):
            at = slice(start, start + CHUNK)
            if again:
                shape = shape_ref[at, :]
            else:
                away = table[2:3, :] - (start + 0.5 * CHUNK)
                shape = steps * (away * (2.0 * SCALE)) + away * away * (-SCALE)
                shape_ref[at, :] = shape
            for n in range(GROUPS):
                score = shape + levels[n]
                g = jnp.exp2(score - (jnp.max(score, axis=1, keepdims=True) - LIFT))
                high, low = halves(g)
                g_high[n, at, :] = high
                g_low[n, at, :] = low.astype(jnp.bfloat16)
            if (start + CHUNK) % PART == 0:
                at = slice(start + CHUNK - PART, start + CHUNK)
                for n in range(GROUPS):
                    found[n].append(product(left_ref[n, 0:rows], g_high[n, at, :], g_low[n, at, :], NT))
        return [jnp.concatenate(parts, axis=1) for parts in found]

    sums = build(False, 16)
    pairs = []
    for n in range(GROUPS):
        found = sums[n]
        inverse = HEAD / (found[0:8] + found[8:16])
        high, low = halves(inverse)
        pairs.append(jnp.concatenate([high.astype(jnp.float32), low], axis=0).astype(jnp.bfloat16))
    total = jnp.zeros((ROWS, columns), jnp.float32)
    for n in range(GROUPS):
        found = product(pairs[n], g_high[n], g_low[n], NN)
        total = total + plain_ref[n] * (found[0:8] + found[8:16])
    rows = total_rows(total) * (1.0 / HEAD)
    shape = (side, side, block)
    inner = lax.broadcasted_iota(jnp.int32, shape, 0) * side + lax.broadcasted_iota(
        jnp.int32, shape, 1
    )
    wanted = [places[m][1] * side + places[m][2] + (side * side) * places[m][0] for m in range(slots)]
    spread = [
        jnp.broadcast_to(rows[0:1, m * block : (m + 1) * block][None], shape) for m in range(slots)
    ]
    for d in range(9):
        found = jnp.zeros(shape, jnp.float32)
        for m in range(slots):
            found = found + jnp.where(inner == wanted[m] - side * side * d, spread[m], 0.0)
        part_send[d // 3, d % 3] = found
    crossing = begin([wide_copy(a, b) for a, b in WIDE])
    extend()
    masses = {(i, j): part_send[i, j] for i in range(3) for j in range(3)}
    for (a, b), one in reversed(list(zip(WIDE, crossing))):
        one.wait_recv()
        a, b = -a, -b
        for i in range(max(a, 0), 3 + min(a, 0)):
            for j in range(max(b, 0), 3 + min(b, 0)):
                masses[i, j] = masses[i, j] + part_recv[(a + 2) * 5 + b + 2, i, j]
    for i in range(3):
        for j in range(3):
            mass = masses[i, j]
            d = 3 * i + j
            mid_all[d] = halo[d, 3] + step_rate * (halo[d, 4] - mass)

    homeward = begin([home_copy(2, mid_all.at[4], mid_home)])
    load_duals(lambda d, r, c: mid_all[d, r, c, :])
    sums = build(True, 10 * ROWS)
    pairs = []
    for n in range(GROUPS):
        found = sums[n]
        inverse = HEAD / (found[0:8] + found[8:16])
        high, low = halves(inverse)
        high = high.astype(jnp.float32)
        low = low.astype(jnp.bfloat16).astype(jnp.float32)
        deep = (high + low) * level_z
        first = deep.astype(jnp.bfloat16).astype(jnp.float32)
        second = (deep - first).astype(jnp.bfloat16).astype(jnp.float32)
        third = deep - first - second
        pairs.append(jnp.concatenate(
            [high, low, first, second, third, jnp.zeros_like(third)], axis=0
        ).astype(jnp.bfloat16))
        inverse = inverse * (1.0 / HEAD)
        offsets = (
            (found[48:56] + found[64:72]) * inverse * -UNIT_XY,
            (found[56:64] + found[72:80]) * inverse * -UNIT_XY,
            ((found[16:24] + found[24:32] + found[32:40]) * inverse - level_z) * HALF_Z,
        )
        for c in range(3):
            for r in range(2):
                disp_send[c, 2 * n + r] = offsets[c][TY * r : TY * r + TY]
        part = (slice(None), pl.ds(2 * n, 2))
        homeward += begin([home_copy(3 + n, disp_send.at[part], disp_ref.at[part])])
    sums = [jnp.zeros((ROWS, columns), jnp.float32) for _ in range(4)]
    for n in range(GROUPS):
        centre_x, centre_y = centres(n)
        found = product(pairs[n], g_high[n], g_low[n], NN)
        plain = plain_ref[n]
        mass = plain * (found[0:8] + found[8:16])
        deep = plain * (found[16:24] + found[24:32] + found[32:40])
        sums[0] = sums[0] + mass
        sums[1] = sums[1] + mass * (centre_x + step_x)
        sums[2] = sums[2] + mass * (centre_y + step_y)
        sums[3] = sums[3] + (deep * HALF_Z - mass * (table[2:3, :] - HALF_Z))
    sums = [total_rows(v) for v in sums]
    kind = serial % 4
    rows = jnp.where(
        kind < 2, jnp.where(kind == 0, sums[0], sums[1]), jnp.where(kind == 2, sums[2], sums[3])
    ) * (1.0 / HEAD)
    upper = lax.broadcasted_iota(jnp.int32, (8, block), 0) // 4
    for d in range(9):
        for v in range(side * side // 2):
            found = jnp.zeros((8, block), jnp.float32)
            for m in range(slots):
                here = upper == wanted[m] - (side * side * d + 2 * v)
                found = found + jnp.where(here, rows[:, m * block : (m + 1) * block], 0.0)
            four_send[d, 8 * v : 8 * v + 8, :] = found
    closing = begin([
        Spread(1, d, wrap(tile + d // 3 - 1), four_send.at[d], four_recv) for d in range(9)
    ])
    for one in listed + opening + crossing:
        one.wait_send()
    four = None
    for d in range(8, -1, -1):
        closing[d].wait()
        four = four_recv[8 - d] if four is None else four + four_recv[8 - d]
    homeward[0].wait()
    for i in range(side * side):
        r, c = i // side, i % side
        goal = mine[4, r, c : c + 1, :]
        found = four[4 * i : 4 * i + 1]
        new_ref[r, c : c + 1, :] = mid_home[r, c : c + 1, :] + step_rate * (goal - found)
        weight = 1.0 / (found + goal)
        for k in range(3):
            shift_ref[k, r, c : c + 1, :] = four[4 * i + k + 1 : 4 * i + k + 2] * weight
    finish(homeward[1:])
    for one in closing:
        one.wait_send()


def place_results(new_ref, shift_ref, disp_ref, new_out, shift_out, disp_out, sems):
    pairs = ((disp_ref, disp_out), (shift_ref, shift_out), (new_ref, new_out))
    copies = [pltpu.make_async_copy(src, dst, sems.at[n]) for n, (src, dst) in enumerate(pairs)]
    for one in copies:
        one.start()
    for one in copies:
        one.wait()


def on_device(site_frac, dual_weight, target_mass, block_list, block_count):
    side = site_frac.shape[1]
    block = site_frac.shape[3]
    columns = block_list.shape[2] * block
    f32, bf16, i32 = jnp.float32, jnp.bfloat16, jnp.int32
    vmem = pl.BlockSpec(memory_space=pltpu.VMEM)
    place = pl.BlockSpec(memory_space=pl.ANY)
    results = pl.pallas_call(
        kernel,
        out_shape=(
            pltpu.VMEM(dual_weight.shape, f32),
            pltpu.VMEM(site_frac.shape, f32),
            pltpu.VMEM((3, TX, TY, Z), f32),
        ),
        in_specs=[place] * 5,
        out_specs=(vmem, vmem, vmem),
        scratch_shapes=[
            pltpu.VMEM((5,) + dual_weight.shape, f32),
            pltpu.VMEM((9, 5) + dual_weight.shape, f32),
            pltpu.VMEM((9,) + dual_weight.shape, f32),
            pltpu.VMEM((3, 3, side, side, block), f32),
            pltpu.VMEM((25, 3, 3, side, side, block), f32),
            pltpu.VMEM((9, 4 * side * side, block), f32),
            pltpu.VMEM((9, 4 * side * side, block), f32),
            pltpu.VMEM((3, TX, TY, Z), f32),
            pltpu.VMEM(dual_weight.shape, f32),
            pltpu.SMEM(block_list.shape, i32),
            pltpu.SMEM(block_count.shape, i32),
            pltpu.SMEM(block_list.shape, i32),
            pltpu.SMEM(block_count.shape, i32),
            pltpu.VMEM((8, columns), f32),
            pltpu.VMEM((8, columns), f32),
            pltpu.VMEM((GROUPS, ROWS, columns), f32),
            pltpu.VMEM((GROUPS, 10 * ROWS, columns), bf16),
            pltpu.VMEM((Z, columns), f32),
            pltpu.VMEM((GROUPS, Z, columns), bf16),
            pltpu.VMEM((GROUPS, Z, columns), bf16),
            pltpu.SemaphoreType.DMA((25,)),
            pltpu.SemaphoreType.DMA((25,)),
            pltpu.SemaphoreType.DMA((2, 9)),
            pltpu.SemaphoreType.DMA((2, 9)),
            pltpu.SemaphoreType.DMA((3 + GROUPS,)),
            pltpu.SemaphoreType.DMA((3 + GROUPS,)),
            pltpu.SemaphoreType.DMA((5,)),
        ],
        compiler_params=pltpu.CompilerParams(collective_id=0, has_side_effects=True),
        name="transport",
    )(site_frac, dual_weight, target_mass, block_list, block_count)
    return pl.pallas_call(
        place_results,
        out_shape=tuple(jax.ShapeDtypeStruct(r.shape, f32) for r in results),
        in_specs=[vmem] * 3,
        out_specs=(pl.BlockSpec(memory_space=pltpu.HBM),) * 3,
        scratch_shapes=[pltpu.SemaphoreType.DMA((3,))],
        name="place",
    )(*[pltpu.with_memory_space_constraint(r, pltpu.VMEM) for r in results])


def solution(mesh):
    in_specs = (
        P(None, "gx", "gy", None),
        P("gx", "gy", None),
        P("gx", "gy", None),
        P("gx", "gy", None),
        P("gx", "gy"),
    )
    out_specs = (P("gx", "gy", None), P(None, "gx", "gy", None), P(None, "gx", "gy", None))
    return jax.shard_map(
        on_device, mesh=mesh, in_specs=in_specs, out_specs=out_specs, check_vma=False
    )
```
